256 devices in a mesh: leaf: 256 (over x, y, z, core).
Axes of the slice: x: 4, y: 4, z: 8, core: 2. Of those that a mesh axis runs over, the one named last changes fastest.
Arguments:
- right_side: bfloat16 [262144, 256], P('leaf'), may hold values from -6 to 6
- leaf_inv: bfloat16 [262144, 1024], P('leaf'), may hold values from -0.1875 to 0.1875
- right_basis: bfloat16 [4, 262144, 256], P(None, 'leaf'), may hold values from -0.0234375 to 0.0234375
- left_basis: bfloat16 [4, 262144, 256], P(None, 'leaf'), may hold values from -0.375 to 0.375
- reduced_first: float32 [512, 512], P('leaf'), may hold values from -0.25 to 0.25
- reduced_second: float32 [1024, 512], P('leaf'), may hold values from -0.25 to 0.25
- reduced_third: float32 [2048, 512], P('leaf'), may hold values from -0.25 to 0.25
- reduced_fourth: float32 [4096, 512], P('leaf'), may hold values from -0.25 to 0.25
Outputs:
- solution: float32 [262144, 256], P('leaf')
The draws below stay inside these ranges and needn't reach their ends.
All inputs are finite; a program needn't handle non-finite values.
Results may differ from the reference program's by a relative error of at most 0.0003.
Values sent between devices are 32-bit elements; how exact they have to be, the bound alone decides.
No kernel may reach another device: no remote copies, remote signals or barrier semaphores. Data moves between devices by JAX's collectives and lax.ppermute only.
A program may use at most 64 MiB of HBM per device.

```python
import jax
import jax.numpy as jnp
from jax import lax

LEAF = 1024
COLS = 256
RANK = 256
LEVELS = 4
UNKNOWNS = 262144
N_LEAF = 256


def shard_levels(own_key, extent, split, least, top_value):
    def one(position, blocks):
        draws = jax.random.uniform(jax.random.fold_in(jax.random.fold_in(own_key, 6), position), (blocks,), jnp.float32, least / len(split), top_value / len(split))
        return jnp.repeat(jnp.exp(draws), extent[position] // blocks).reshape((-1,) + (1,) * (len(extent) - position - 1))

    loudness = one(*split[0])
    for cut in split[1:]:
        loudness = loudness * one(*cut)
    return loudness


def noise(stream_key, extent, deviation, limit, cuts=(), kind=jnp.bfloat16):
    gain = shard_levels(stream_key, extent, cuts, -0.22, 0.18) if cuts else 1.0
    result = jax.random.normal(stream_key, extent, jnp.float32) * deviation * gain
    return jnp.minimum(jnp.maximum(result, -limit), limit).astype(kind)


def setup_inputs(seed: int = 0) -> dict:
    key_of = jax.random.split(jax.random.key(seed), 9)
    return {
        "right_side": noise(key_of[0], (UNKNOWNS, COLS), 1.0, 6.0, ((0, 256),)),
        "leaf_inv": noise(key_of[1], (UNKNOWNS, LEAF), LEAF ** -0.5, 0.1875, ((0, 256),)),
        "right_basis": noise(key_of[2], (LEVELS, UNKNOWNS, RANK), (LEAF * N_LEAF // 4) ** -0.5, 0.0234375, ((1, 256),)),
        "left_basis": noise(key_of[3], (LEVELS, UNKNOWNS, RANK), RANK ** -0.5, 0.375, ((1, 256),)),
        "reduced_first": noise(key_of[4], (RANK * 2, 2 * RANK), (2 * RANK) ** -0.5, 0.25, ((0, 256),), jnp.float32),
        "reduced_second": noise(key_of[5], (RANK * 4, 2 * RANK), (2 * RANK) ** -0.5, 0.25, ((0, 256),), jnp.float32),
        "reduced_third": noise(key_of[6], (RANK * 8, 2 * RANK), (2 * RANK) ** -0.5, 0.25, ((0, 256),), jnp.float32),
        "reduced_fourth": noise(key_of[7], (RANK * 16, 2 * RANK), (2 * RANK) ** -0.5, 0.25, ((0, 256),), jnp.float32),
    }


def leaf_apply(pair):
    return jnp.dot(pair[0], pair[1], preferred_element_type=jnp.float32)


def reference(right_side, leaf_inv, right_basis, left_basis, reduced_first, reduced_second, reduced_third, reduced_fourth):
    devices_all = N_LEAF
    blocks = right_side.reshape(devices_all, LEAF, COLS)
    inverses = leaf_inv.reshape(devices_all, LEAF, LEAF)
    solution = lax.map(leaf_apply, (inverses, blocks))
    reduced_all = (reduced_first, reduced_second, reduced_third, reduced_fourth)
    for level in range(LEVELS, 0, -1):
        children = 2 ** level
        child_size = devices_all // children
        right_rows = right_basis[level - 1].reshape(devices_all, LEAF, RANK).astype(jnp.float32)
        partial_value = jnp.einsum("dlr,dlc->drc", right_rows, solution, precision=lax.Precision.HIGHEST)
        sums = partial_value.reshape(children, child_size, RANK, COLS).sum(axis=1)
        stacked = sums.reshape(children // 2, 2 * RANK, COLS)
        reduced = reduced_all[level - 1].reshape(children // 2, 2 * RANK, 2 * RANK)
        mixed = jnp.einsum("nij,njc->nic", reduced, stacked, precision=lax.Precision.HIGHEST)
        mixed = mixed.reshape(children, RANK, COLS)
        per_device = jnp.repeat(mixed, child_size, axis=0)
        left_rows = left_basis[level - 1].reshape(devices_all, LEAF, RANK).astype(jnp.float32)
        solution = solution - jnp.einsum("dlr,drc->dlc", left_rows, per_device, precision=lax.Precision.HIGHEST)
    return solution.reshape(devices_all * LEAF, COLS)
```

```python
import jax
import jax.numpy as jnp
from jax import lax
from jax.sharding import Mesh, PartitionSpec as P

LEVELS = 4
AXES = ("xh", "xl", "yh", "yl", "z", "c")
SIZES = (2, 2, 2, 2, 8, 2)
Z = 8
HIGHEST = lax.Precision.HIGHEST
F32 = jnp.float32


def split(value):
    high = lax.reduce_precision(value, 8, 7)
    return high.astype(jnp.bfloat16), (value - high).astype(jnp.bfloat16)


def dot(a, b, dims):
    return lax.dot_general(a, b, ((dims[0], dims[1]), ((), ())), preferred_element_type=F32)


def fdot(a, b, dims):
    return lax.dot_general(a, b, ((dims[0], dims[1]), ((), ())), precision=HIGHEST, preferred_element_type=F32)


def exchange(block, axes):
    return lax.all_to_all(block, axes, 0, 0, tiled=True)


def swap_core(block):
    return lax.ppermute(block, "c", [(0, 1), (1, 0)])


def spread(block, axes, count):
    full = jnp.broadcast_to(block[None], (count,) + block.shape)
    return exchange(full, axes)


def scatter_sum(blocks, core):
    n = blocks.shape[0]
    halves = blocks.reshape(n, 2, 128, 256)
    give = jnp.where(core == 0, halves[:, 1], halves[:, 0])
    keep = jnp.where(core == 0, halves[:, 0], halves[:, 1])
    mine = keep + swap_core(give)
    mine = mine.reshape(n, Z, 16, 256).transpose(1, 0, 2, 3)
    return exchange(mine, "z").sum(axis=0)


def gather_rows(block, core):
    n = block.shape[0]
    half = spread(block, "z", Z).transpose(1, 0, 2, 3).reshape(n, 128, 256)
    other = swap_core(half)
    low = jnp.where(core == 0, half, other)
    high = jnp.where(core == 0, other, half)
    return jnp.concatenate([low, high], axis=1)


def local(right_side, leaf_inv, right_basis, left_basis, k1, k2, k3, k4):
    core = lax.axis_index("c")
    rows = jnp.concatenate([k4, k3, k2, k1, jnp.zeros((2, 512), F32)], axis=0)
    by_z = spread(rows, "z", Z)
    part4 = by_z[:, 0:16]
    part3 = spread(by_z[:, 16:24], "yl", 2)
    part2 = spread(by_z[:, 24:28], ("yh", "yl"), 4)
    part1 = spread(by_z[:, 28:30], ("xl", "yh", "yl"), 8)

    def whole(part):
        other = swap_core(part)
        low = jnp.where(core == 0, part, other)
        high = jnp.where(core == 0, other, part)
        return jnp.stack([low, high], axis=-3).reshape(256, 512)

    x0 = dot(leaf_inv, right_side, ((1,), (0,)))
    hi, lo = split(x0)
    hilo = jnp.concatenate([hi, lo], axis=1)

    def project(j):
        both = dot(hilo, right_basis[j - 1], ((0,), (0,)))
        return both[:256] + both[256:]

    def couple(j, k):
        return dot(left_basis[k - 1], right_basis[j - 1], ((0,), (0,)))

    first = jnp.stack([project(4), couple(3, 4)])
    rest = jnp.stack(
        [project(3), project(2), project(1), couple(2, 4), couple(2, 3), couple(1, 4), couple(1, 3), couple(1, 2)]
    )
    first = scatter_sum(first, core)
    rest = scatter_sum(rest, core)
    p4, g34 = first[0], first[1]
    p3, p2, p1 = rest[0], rest[1], rest[2]
    g34 = gather_rows(g34[None], core)[0]
    g2_1 = gather_rows(rest[3:8], core)
    g24, g23, g14, g13, g12 = [g2_1[n] for n in range(5)]

    def mix(part, stack):
        return fdot(stack, whole(part), ((1,), (1,)))

    def times(m, g):
        return fdot(m, g, ((1,), (0,)))

    def sums(t, axes, count):
        got = spread(t, axes, count).reshape(2, count // 2, 16, 256).sum(axis=1)
        return jnp.concatenate([got[0], got[1]], axis=1)

    m4 = mix(part4, sums(p4, "yl", 2))
    t3 = p3 - times(m4, g34)
    m3 = mix(part3, sums(t3, ("yh", "yl"), 4))
    t2 = p2 - times(m4, g24) - times(m3, g23)
    m2 = mix(part2, sums(t2, ("xl", "yh", "yl"), 8))
    t1 = p1 - times(m4, g14) - times(m3, g13) - times(m2, g12)
    m1 = mix(part1, sums(t1, ("xh", "xl", "yh", "yl"), 16))

    def correction(m, level):
        mh, ml = split(m)
        left = left_basis[level - 1]
        return dot(left, mh, ((1,), (1,))) + dot(left, ml, ((1,), (1,)))

    late = gather_rows(jnp.stack([m4, m3, m2]), core)
    out = x0 - correction(late[0], 4) - correction(late[1], 3) - correction(late[2], 2)
    last = gather_rows(m1[None], core)
    return out - correction(last[0], 1)


def solution(mesh):
    fine = Mesh(mesh.devices.reshape(SIZES), AXES)
    row = P(AXES, None)
    level = P(None, AXES, None)
    return jax.shard_map(
        local,
        mesh=fine,
        in_specs=(row, row, level, level, row, row, row, row),
        out_specs=row,
        check_vma=False,
    )
```

```python
import jax
import jax.numpy as jnp
from jax import lax
from jax.experimental import pallas as pl
from jax.experimental.pallas import tpu as pltpu
from jax.sharding import Mesh, PartitionSpec as P

AXES = ("xh", "xl", "yh", "yl", "z", "c")
SIZES = (2, 2, 2, 2, 8, 2)
Z = 8
STEPS = 4
F32 = jnp.float32
BF16 = jnp.bfloat16
PAIRS = ((3, 4), (2, 4), (2, 3), (1, 4), (1, 3), (1, 2))


def split(value):
    high = lax.reduce_precision(value, 8, 7)
    return high.astype(BF16), (value - high).astype(BF16)


def dot(a, b, dims):
    return lax.dot_general(a, b, ((dims[0], dims[1]), ((), ())), preferred_element_type=F32)


def fdot(a, b, dims):
    return lax.dot_general(
        a, b, ((dims[0], dims[1]), ((), ())), precision=lax.Precision.HIGH, preferred_element_type=F32
    )


def leaf_kernel(core_ref, inv_ref, rhs_ref, v_ref, w_ref, x_ref, out_ref, acc_ref):
    step = pl.program_id(0)
    x = jnp.dot(inv_ref[...], rhs_ref[...], preferred_element_type=F32)
    x_ref[...] = x
    high = x.astype(BF16)
    low = (x - high.astype(F32)).astype(BF16)

    def add(n, value):
        @pl.when(step == 0)
        def _():
            acc_ref[n] = value

        @pl.when(step > 0)
        def _():
            acc_ref[n] = acc_ref[n] + value

    for n, j in enumerate((4, 3, 2, 1)):
        v = v_ref[j - 1]
        add(n, dot(high, v, ((0,), (0,))) + dot(low, v, ((0,), (0,))))
    for n, (j, k) in enumerate(PAIRS):
        add(4 + n, dot(w_ref[k - 1], v_ref[j - 1], ((0,), (0,))))

    @pl.when(step == STEPS - 1)
    def _():
        core = core_ref[0]
        for half in range(2):
            slot = jnp.where(core == half, 0, 1)
            for z in range(Z):
                start = half * 128 + z * 16
                out_ref[slot, z] = acc_ref[:, start : start + 16, :]


def leaf(core, leaf_inv, right_side, right_basis, left_basis):
    rows = 1024 // STEPS
    return pl.pallas_call(
        leaf_kernel,
        grid_spec=pltpu.PrefetchScalarGridSpec(
            num_scalar_prefetch=1,
            grid=(STEPS,),
            in_specs=[
                pl.BlockSpec((rows, 1024), lambda s, c: (s, 0)),
                pl.BlockSpec((1024, 256), lambda s, c: (0, 0)),
                pl.BlockSpec((4, rows, 256), lambda s, c: (0, s, 0)),
                pl.BlockSpec((4, rows, 256), lambda s, c: (0, s, 0)),
            ],
            out_specs=[
                pl.BlockSpec((rows, 256), lambda s, c: (s, 0)),
                pl.BlockSpec((2, Z, 10, 16, 256), lambda s, c: (0, 0, 0, 0, 0)),
            ],
            scratch_shapes=[pltpu.VMEM((10, 256, 256), F32)],
        ),
        out_shape=[
            jax.ShapeDtypeStruct((1024, 256), F32),
            jax.ShapeDtypeStruct((2, Z, 10, 16, 256), F32),
        ],
    )(core.reshape(1), leaf_inv, right_side, right_basis, left_basis)


def partner(block, axis):
    return lax.ppermute(block, axis, [(0, 1), (1, 0)])


def ordered(bit, own, other, axis):
    low = jnp.where(bit == 0, own, other)
    high = jnp.where(bit == 0, other, own)
    return jnp.concatenate([low, high], axis=axis)


def exchange(block, axes):
    return lax.all_to_all(block, axes, 0, 0, tiled=True)


def spread(block, axes, count):
    return exchange(jnp.broadcast_to(block[None], (count,) + block.shape), axes)


def local(right_side, leaf_inv, right_basis, left_basis, k1, k2, k3, k4):
    at = {axis: lax.axis_index(axis) for axis in AXES}
    core = at["c"]
    rows = spread(jnp.concatenate([k4, k3, k2, k1, jnp.zeros((2, 512), F32)], axis=0), "z", Z)
    part4, part3, part2, part1 = rows[:, 0:16], rows[None, :, 16:24], rows[None, :, 24:28], rows[None, :, 28:30]

    def widen(part, axis):
        return ordered(at[axis], part, partner(part, axis), 0)

    part3 = widen(part3, "yl")
    part2 = widen(widen(part2, "yl"), "yh")
    part1 = widen(widen(widen(part1, "yl"), "yh"), "xl")

    def whole(part):
        other = partner(part, "c")
        low = jnp.where(core == 0, part, other)
        high = jnp.where(core == 0, other, part)
        return jnp.stack([low, high], axis=-3).reshape(256, 512)

    x0, sums = leaf(core, leaf_inv, right_side, right_basis, left_basis)
    sums = exchange(sums[0] + partner(sums[1], "c"), "z").sum(axis=0)
    p4, p3, p2, p1 = sums[0], sums[1], sums[2], sums[3]

    def both_cores(by_z):
        n = by_z.shape[1]
        half = by_z.transpose(1, 0, 2, 3).reshape(n, 128, 256)
        return ordered(core, half, partner(half, "c"), 1)

    g_a = both_cores(spread(sums[4:7], "z", Z))
    g_b = both_cores(spread(sums[7:10], "z", Z))

    def mix(part, own, other, axis):
        stack = ordered(at[axis], own, other, 1)
        return fdot(stack, whole(part), ((1,), (1,)))

    def times(m, g):
        return fdot(m, g, ((1,), (0,)))

    def total(t, axes):
        for axis in axes:
            t = t + partner(t, axis)
        return t

    m4 = mix(part4, p4, partner(p4, "yl"), "yl")
    s3 = total(p3 - times(m4, g_a[0]), ("yl",))
    m3 = mix(part3, s3, partner(s3, "yh"), "yh")
    t2 = p2 - times(m4, g_a[1]) - times(m3, g_a[2])
    early = spread(jnp.stack([m4, m3]), "z", Z)
    s2 = total(t2, ("yl", "yh"))
    s2, early = lax.optimization_barrier((s2, early))
    m2 = mix(part2, s2, partner(s2, "xl"), "xl")
    t1 = p1 - times(m4, g_b[0]) - times(m3, g_b[1]) - times(m2, g_b[2])
    s1 = spread(t1, ("xh", "xl", "yh", "yl"), 16).reshape(2, 8, 16, 256).sum(axis=1)
    m1 = fdot(jnp.concatenate([s1[0], s1[1]], axis=1), whole(part1), ((1,), (1,)))

    def correction(m, level):
        mh, ml = split(m)
        left = left_basis[level - 1]
        return dot(left, mh, ((1,), (1,))) + dot(left, ml, ((1,), (1,)))

    early = both_cores(early)
    out = x0 - correction(early[0], 4) - correction(early[1], 3)
    last = both_cores(spread(jnp.stack([m2, m1]), "z", Z))
    return out - correction(last[0], 2) - correction(last[1], 1)


def solution(mesh):
    fine = Mesh(mesh.devices.reshape(SIZES), AXES)
    row = P(AXES, None)
    level = P(None, AXES, None)
    return jax.shard_map(
        local,
        mesh=fine,
        in_specs=(row, row, level, level, row, row, row, row),
        out_specs=row,
        check_vma=False,
    )
```

```python
import jax
import jax.numpy as jnp
from jax import lax
from jax.experimental import pallas as pl
from jax.experimental.pallas import tpu as pltpu
from jax.sharding import Mesh, PartitionSpec as P

AXES = ("xh", "xl", "yh", "yl", "z", "c")
SIZES = (2, 2, 2, 2, 8, 2)
Z = 8
STEPS = 4
F32 = jnp.float32
BF16 = jnp.bfloat16
PAIRS = ((3, 4), (2, 4), (1, 4), (2, 3), (1, 3), (1, 2))


def dot(a, b, dims):
    return lax.dot_general(a, b, ((dims[0], dims[1]), ((), ())), preferred_element_type=F32)


def fdot(a, b, dims):
    return lax.dot_general(
        a, b, ((dims[0], dims[1]), ((), ())), precision=lax.Precision.HIGH, preferred_element_type=F32
    )


def pack_kernel(a_ref, b_ref, c_ref, d_ref, out_ref):
    for z in range(Z):
        out_ref[z, 0:16, :] = a_ref[...]
        out_ref[z, 16:24, :] = b_ref[...]
        out_ref[z, 24:28, :] = c_ref[...]
        out_ref[z, 28:30, :] = d_ref[...]
        out_ref[z, 30:32, :] = jnp.zeros((2, 512), F32)


def pack(k4, k3, k2, k1):
    return pl.pallas_call(pack_kernel, out_shape=jax.ShapeDtypeStruct((Z, 32, 512), F32), name="pack")(k4, k3, k2, k1)


def leaf_kernel(core_ref, inv_hbm, rhs_hbm, v_hbm, w_hbm, x_ref, keep_ref, give_ref, inv_ref, rhs_ref, v_ref, w_ref, high_ref, low_ref, sems):
    rows = 1024 // STEPS
    count = [0]

    def load(src, dst):
        copy = pltpu.make_async_copy(src, dst, sems.at[count[0]])
        count[0] += 1
        copy.start()
        return copy

    wait_w, wait_v = {}, {}
    wait_w[4] = load(w_hbm.at[3], w_ref.at[2])
    wait_v[3] = load(v_hbm.at[2], v_ref.at[2])
    wait_v[2] = load(v_hbm.at[1], v_ref.at[1])
    wait_v[1] = load(v_hbm.at[0], v_ref.at[0])
    wait_w[3] = load(w_hbm.at[2], w_ref.at[1])
    wait_w[2] = load(w_hbm.at[1], w_ref.at[0])
    wait_rhs = load(rhs_hbm, rhs_ref)
    parts = [pl.ds(step * rows, rows) for step in range(STEPS)]
    wait_inv = [load(inv_hbm.at[part], inv_ref.at[part]) for part in parts]
    wait_v[4] = load(v_hbm.at[3], v_ref.at[3])
    first = core_ref[0] == 0

    def store(n, value):
        low, high = value[:128], value[128:]
        keep_ref[:, n] = jnp.where(first, low, high).reshape(Z, 16, 256)
        give_ref[:, n] = jnp.where(first, high, low).reshape(Z, 16, 256)

    done = set()

    def ready(waits, level):
        if (id(waits), level) not in done:
            done.add((id(waits), level))
            waits[level].wait()

    turned = {}
    for n, (j, k) in enumerate(PAIRS):
        ready(wait_w, k)
        if k not in turned:
            turned[k] = w_ref[k - 2].T
        ready(wait_v, j)
        store(4 + n, dot(turned[k], v_ref[j - 1], ((1,), (0,))))
    wait_rhs.wait()
    rhs = rhs_ref[...]
    rhs_turned = rhs.T
    for step, part in enumerate(parts):
        wait_inv[step].wait()
        inv = inv_ref[part, :]
        x_ref[part, :] = jnp.dot(inv, rhs, preferred_element_type=F32)
        xt = dot(rhs_turned, inv, ((1,), (1,)))
        high = xt.astype(BF16)
        high_ref[:, part] = high
        low_ref[:, part] = (xt - high.astype(F32)).astype(BF16)
    for n, j in enumerate((4, 3, 2, 1)):
        ready(wait_v, j)
        v = v_ref[j - 1]
        store(n, dot(high_ref[...], v, ((1,), (0,))) + dot(low_ref[...], v, ((1,), (0,))))


def leaf(core, leaf_inv, right_side, right_basis, left_basis):
    any_space = pl.BlockSpec(memory_space=pl.ANY)
    return pl.pallas_call(
        leaf_kernel,
        in_specs=[pl.BlockSpec(memory_space=pltpu.SMEM)] + [any_space] * 4,
        out_shape=[
            jax.ShapeDtypeStruct((1024, 256), F32),
            jax.ShapeDtypeStruct((Z, 10, 16, 256), F32),
            jax.ShapeDtypeStruct((Z, 10, 16, 256), F32),
        ],
        scratch_shapes=[
            pltpu.VMEM((1024, 1024), BF16),
            pltpu.VMEM((1024, 256), BF16),
            pltpu.VMEM((4, 1024, 256), BF16),
            pltpu.VMEM((3, 1024, 256), BF16),
            pltpu.VMEM((256, 1024), BF16),
            pltpu.VMEM((256, 1024), BF16),
            pltpu.SemaphoreType.DMA((8 + STEPS,)),
        ],
        name="leaf",
    )(core.reshape(1), leaf_inv, right_side, right_basis, left_basis)


def finish_kernel(core_ref, w_ref, x_ref, own_ref, other_ref, out_ref, high_ref, low_ref):
    first = core_ref[0] == 0

    @pl.when(pl.program_id(0) == 0)
    def _():
        for n in range(4):
            own = own_ref[:, n].reshape(128, 256)
            other = other_ref[:, n].reshape(128, 256)
            m = jnp.concatenate([jnp.where(first, own, other), jnp.where(first, other, own)], axis=0)
            high = m.astype(BF16)
            high_ref[n] = high
            low_ref[n] = (m - high.astype(F32)).astype(BF16)

    total = x_ref[...]
    for n, level in enumerate((4, 3, 2, 1)):
        w = w_ref[level - 1]
        total = total - (dot(w, high_ref[n], ((1,), (1,))) + dot(w, low_ref[n], ((1,), (1,))))
    out_ref[...] = total


def finish(core, left_basis, x, own, other):
    rows = 1024 // STEPS
    whole = pl.BlockSpec((Z, 4, 16, 256), lambda s: (0, 0, 0, 0))
    return pl.pallas_call(
        finish_kernel,
        grid=(STEPS,),
        in_specs=[
            pl.BlockSpec(memory_space=pltpu.SMEM),
            pl.BlockSpec((4, rows, 256), lambda s: (0, s, 0)),
            pl.BlockSpec((rows, 256), lambda s: (s, 0)),
            whole,
            whole,
        ],
        out_specs=pl.BlockSpec((rows, 256), lambda s: (s, 0)),
        out_shape=jax.ShapeDtypeStruct((1024, 256), F32),
        scratch_shapes=[pltpu.VMEM((4, 256, 256), BF16), pltpu.VMEM((4, 256, 256), BF16)],
        name="finish",
    )(core.reshape(1), left_basis, x, own, other)


def partner(block, axis):
    return lax.ppermute(block, axis, [(0, 1), (1, 0)])


def ordered(bit, own, other, axis):
    low = jnp.where(bit == 0, own, other)
    high = jnp.where(bit == 0, other, own)
    return jnp.concatenate([low, high], axis=axis)


def exchange(block, axes):
    return lax.all_to_all(block, axes, 0, 0, tiled=True)


def spread(block, axes, count):
    return exchange(jnp.broadcast_to(block[None], (count,) + block.shape), axes)


def local(right_side, leaf_inv, right_basis, left_basis, k1, k2, k3, k4):
    at = {axis: lax.axis_index(axis) for axis in AXES}
    core = at["c"]
    rows = exchange(pack(k4, k3, k2, k1), "z")
    x0, keep, give = leaf(core, leaf_inv, right_side, right_basis, left_basis)
    mine, rows = lax.optimization_barrier((keep + partner(give, "c"), rows))
    sums = exchange(mine, "z").sum(axis=0)

    part4, part3, part2, part1 = rows[:, 0:16], rows[None, :, 16:24], rows[None, :, 24:28], rows[None, :, 28:30]

    def widen(part, axis):
        return ordered(at[axis], part, partner(part, axis), 0)

    part3 = widen(part3, "yl")
    part2 = widen(widen(part2, "yl"), "yh")
    part1 = widen(widen(widen(part1, "yl"), "yh"), "xl")
    other4 = partner(part4, "c")

    def whole(part, other=None):
        if other is None:
            other = partner(part, "c")
        low = jnp.where(core == 0, part, other)
        high = jnp.where(core == 0, other, part)
        return jnp.stack([low, high], axis=-3).reshape(256, 512)

    def both_cores(by_z):
        n = by_z.shape[1]
        half = by_z.transpose(1, 0, 2, 3).reshape(n, 128, 256)
        return ordered(core, half, partner(half, "c"), 1)

    def mix(part, own, axis, other=None):
        stack = ordered(at[axis], own, partner(own, axis), 1)
        return fdot(stack, whole(part, other), ((1,), (1,)))

    def times(m, g):
        return fdot(m, g, ((1,), (0,)))

    g34, g24, g14 = both_cores(spread(sums[4:7], "z", Z))
    shared = sums[7:10]
    shared = shared + partner(shared, "yl")
    shared = jnp.concatenate([shared[:2], shared[2:] + partner(shared[2:], "yh")], axis=0)
    m4 = mix(part4, sums[0], "yl", other4)
    t = sums[1:4] - jnp.stack([times(m4, g34), times(m4, g24), times(m4, g14)])
    g23, g13, g12 = both_cores(spread(shared, "z", Z))
    t = t + partner(t, "yl")
    m3 = mix(part3, t[0], "yh")
    t = t[1:] - jnp.stack([times(m3, g23), times(m3, g13)])
    t = t + partner(t, "yh")
    m2 = mix(part2, t[0], "xl")
    t = t[1] - times(m2, g12)
    t = t + partner(t, "xl")
    m1 = mix(part1, t, "xh")

    last = spread(jnp.stack([m4, m3, m2, m1]), "z", Z)
    return finish(core, left_basis, x0, last, partner(last, "c"))


def solution(mesh):
    fine = Mesh(mesh.devices.reshape(SIZES), AXES)
    row = P(AXES, None)
    level = P(None, AXES, None)
    return jax.shard_map(
        local,
        mesh=fine,
        in_specs=(row, row, level, level, row, row, row, row),
        out_specs=row,
        check_vma=False,
    )
```

```python
import jax
import jax.numpy as jnp
from jax import lax
from jax.experimental import pallas as pl
from jax.experimental.pallas import tpu as pltpu
from jax.sharding import Mesh, PartitionSpec as P

AXES = ("xh", "xl", "yh", "yl", "z", "c")
SIZES = (2, 2, 2, 2, 8, 2)
Z = 8
STEPS = 4
F32 = jnp.float32
BF16 = jnp.bfloat16
PAIRS = ((3, 4), (2, 4), (1, 4), (2, 3), (1, 3), (1, 2))
DIRECT = (4, (3, 4), (2, 4), (1, 4))
SHARED = (3, (2, 3), (1, 3), 2, 1, (1, 2))


def dot(a, b, dims):
    return lax.dot_general(a, b, ((dims[0], dims[1]), ((), ())), preferred_element_type=F32)


def fdot(a, b, dims):
    return lax.dot_general(
        a, b, ((dims[0], dims[1]), ((), ())), precision=lax.Precision.HIGH, preferred_element_type=F32
    )


def pack_kernel(a_ref, b_ref, c_ref, d_ref, out_ref):
    for z in range(Z):
        out_ref[z, 0:16, :] = a_ref[...]
        out_ref[z, 16:24, :] = b_ref[...]
        out_ref[z, 24:28, :] = c_ref[...]
        out_ref[z, 28:30, :] = d_ref[...]
        out_ref[z, 30:32, :] = jnp.zeros((2, 512), F32)


def pack(k4, k3, k2, k1):
    return pl.pallas_call(pack_kernel, out_shape=jax.ShapeDtypeStruct((Z, 32, 512), F32), name="pack")(k4, k3, k2, k1)


def leaf_kernel(
    place_ref, inv_hbm, rhs_hbm, v_hbm, w_hbm, x_ref, keep_ref, give_ref, keep_shared_ref, give_shared_ref,
    inv_ref, rhs_ref, v_ref, w_ref, high_ref, low_ref, sems,
):
    rows = 1024 // STEPS
    count = [0]

    def load(src, dst):
        copy = pltpu.make_async_copy(src, dst, sems.at[count[0]])
        count[0] += 1
        copy.start()
        return copy

    wait_w, wait_v = {}, {}
    wait_w[4] = load(w_hbm.at[3], w_ref.at[2])
    wait_v[3] = load(v_hbm.at[2], v_ref.at[2])
    wait_v[2] = load(v_hbm.at[1], v_ref.at[1])
    wait_v[1] = load(v_hbm.at[0], v_ref.at[0])
    wait_w[3] = load(w_hbm.at[2], w_ref.at[1])
    wait_w[2] = load(w_hbm.at[1], w_ref.at[0])
    wait_rhs = load(rhs_hbm, rhs_ref)
    parts = [pl.ds(step * rows, rows) for step in range(STEPS)]
    wait_inv = [load(inv_hbm.at[part], inv_ref.at[part]) for part in parts]
    wait_v[4] = load(v_hbm.at[3], v_ref.at[3])
    first_core = place_ref[0] == 0
    first_lanes = place_ref[1] == 0

    def store(name, value):
        low, high = value[:128], value[128:]
        keep = jnp.where(first_core, low, high).reshape(Z, 16, 256)
        give = jnp.where(first_core, high, low).reshape(Z, 16, 256)
        if name in DIRECT:
            keep_ref[:, DIRECT.index(name)] = keep
            give_ref[:, DIRECT.index(name)] = give
            return
        n = SHARED.index(name)
        for value, ref in ((keep, keep_shared_ref), (give, give_shared_ref)):
            left, right = value[:, :, :128], value[:, :, 128:]
            ref[0, :, n] = jnp.where(first_lanes, left, right)
            ref[1, :, n] = jnp.where(first_lanes, right, left)

    done = set()

    def ready(waits, level):
        if (id(waits), level) not in done:
            done.add((id(waits), level))
            waits[level].wait()

    turned = {}
    for j, k in PAIRS:
        ready(wait_w, k)
        if k not in turned:
            turned[k] = w_ref[k - 2].T
        ready(wait_v, j)
        store((j, k), dot(turned[k], v_ref[j - 1], ((1,), (0,))))
    wait_rhs.wait()
    rhs = rhs_ref[...]
    rhs_turned = rhs.T
    for step, part in enumerate(parts):
        wait_inv[step].wait()
        inv = inv_ref[part, :]
        x_ref[part, :] = jnp.dot(inv, rhs, preferred_element_type=F32)
        xt = dot(rhs_turned, inv, ((1,), (1,)))
        high = xt.astype(BF16)
        high_ref[:, part] = high
        low_ref[:, part] = (xt - high.astype(F32)).astype(BF16)
    for j in (4, 3, 2, 1):
        ready(wait_v, j)
        v = v_ref[j - 1]
        store(j, dot(high_ref[...], v, ((1,), (0,))) + dot(low_ref[...], v, ((1,), (0,))))


def leaf(place, leaf_inv, right_side, right_basis, left_basis):
    any_space = pl.BlockSpec(memory_space=pl.ANY)
    return pl.pallas_call(
        leaf_kernel,
        in_specs=[pl.BlockSpec(memory_space=pltpu.SMEM)] + [any_space] * 4,
        out_shape=[
            jax.ShapeDtypeStruct((1024, 256), F32),
            jax.ShapeDtypeStruct((Z, 4, 16, 256), F32),
            jax.ShapeDtypeStruct((Z, 4, 16, 256), F32),
            jax.ShapeDtypeStruct((2, Z, 6, 16, 128), F32),
            jax.ShapeDtypeStruct((2, Z, 6, 16, 128), F32),
        ],
        scratch_shapes=[
            pltpu.VMEM((1024, 1024), BF16),
            pltpu.VMEM((1024, 256), BF16),
            pltpu.VMEM((4, 1024, 256), BF16),
            pltpu.VMEM((3, 1024, 256), BF16),
            pltpu.VMEM((256, 1024), BF16),
            pltpu.VMEM((256, 1024), BF16),
            pltpu.SemaphoreType.DMA((8 + STEPS,)),
        ],
        name="leaf",
    )(place, leaf_inv, right_side, right_basis, left_basis)


def finish_kernel(core_ref, w_ref, x_ref, own_ref, other_ref, out_ref, high_ref, low_ref):
    first = core_ref[0] == 0

    @pl.when(pl.program_id(0) == 0)
    def _():
        for n in range(4):
            own = own_ref[:, n].reshape(128, 256)
            other = other_ref[:, n].reshape(128, 256)
            m = jnp.concatenate([jnp.where(first, own, other), jnp.where(first, other, own)], axis=0)
            high = m.astype(BF16)
            high_ref[n] = high
            low_ref[n] = (m - high.astype(F32)).astype(BF16)

    total = x_ref[...]
    for n, level in enumerate((4, 3, 2, 1)):
        w = w_ref[level - 1]
        total = total - (dot(w, high_ref[n], ((1,), (1,))) + dot(w, low_ref[n], ((1,), (1,))))
    out_ref[...] = total


def finish(core, left_basis, x, own, other):
    rows = 1024 // STEPS
    whole = pl.BlockSpec((Z, 4, 16, 256), lambda s: (0, 0, 0, 0))
    return pl.pallas_call(
        finish_kernel,
        grid=(STEPS,),
        in_specs=[
            pl.BlockSpec(memory_space=pltpu.SMEM),
            pl.BlockSpec((4, rows, 256), lambda s: (0, s, 0)),
            pl.BlockSpec((rows, 256), lambda s: (s, 0)),
            whole,
            whole,
        ],
        out_specs=pl.BlockSpec((rows, 256), lambda s: (s, 0)),
        out_shape=jax.ShapeDtypeStruct((1024, 256), F32),
        scratch_shapes=[pltpu.VMEM((4, 256, 256), BF16), pltpu.VMEM((4, 256, 256), BF16)],
        name="finish",
    )(core.reshape(1), left_basis, x, own, other)


def partner(block, axis):
    return lax.ppermute(block, axis, [(0, 1), (1, 0)])


def ordered(bit, own, other, axis):
    low = jnp.where(bit == 0, own, other)
    high = jnp.where(bit == 0, other, own)
    return jnp.concatenate([low, high], axis=axis)


def exchange(block, axes):
    return lax.all_to_all(block, axes, 0, 0, tiled=True)


def spread(block, axes, count):
    return exchange(jnp.broadcast_to(block[None], (count,) + block.shape), axes)


def local(right_side, leaf_inv, right_basis, left_basis, k1, k2, k3, k4):
    at = {axis: lax.axis_index(axis) for axis in AXES}
    core = at["c"]
    rows = exchange(pack(k4, k3, k2, k1), "z")
    x0, keep, give, keep_shared, give_shared = leaf(
        jnp.stack([core, at["yl"]]), leaf_inv, right_side, right_basis, left_basis
    )
    mine = keep + partner(give, "c")
    got_shared = partner(give_shared, "c")
    got = partner(keep_shared[1] + got_shared[1], "yl")
    direct = exchange(mine, "z")
    pairs = (keep_shared[0] + got_shared[0]) + got
    upper = at["yh"] == 0
    fours = pairs[:, 3:]
    got = partner(jnp.where(upper, fours[:, :, 8:], fours[:, :, :8]), "yh")
    fours = jnp.where(upper, fours[:, :, :8], fours[:, :, 8:]) + got
    got, rows = lax.optimization_barrier((got, rows))
    part4, part3, part2, part1 = rows[:, 0:16], rows[None, :, 16:24], rows[None, :, 24:28], rows[None, :, 28:30]

    def widen(part, axis):
        return ordered(at[axis], part, partner(part, axis), 0)

    part3 = widen(part3, "yl")
    part2 = widen(widen(part2, "yl"), "yh")
    part1 = widen(widen(widen(part1, "yl"), "yh"), "xl")
    other4 = partner(part4, "c")

    def whole(part, other=None):
        if other is None:
            other = partner(part, "c")
        low = jnp.where(core == 0, part, other)
        high = jnp.where(core == 0, other, part)
        return jnp.stack([low, high], axis=-3).reshape(256, 512)

    def both_cores(own, other, first, count):
        own = own[:, first : first + count].reshape(Z * count, -1)
        other = other[:, first : first + count].reshape(Z * count, -1)
        return ordered(core, own, other, 0)

    def mix(part, own, axis, other=None):
        stack = ordered(at[axis], own, partner(own, axis), 1)
        return fdot(stack, whole(part, other), ((1,), (1,)))

    def times(m, g):
        return fdot(m, g, ((1,), (0,)))

    def in_lanes(block):
        zero = jnp.zeros_like(block)
        first = at["yl"] == 0
        return jnp.concatenate([jnp.where(first, block, zero), jnp.where(first, zero, block)], axis=1)

    def in_rows(block):
        zero = jnp.zeros_like(block)
        return jnp.concatenate([jnp.where(upper, block, zero), jnp.where(upper, zero, block)], axis=0)

    direct = direct.sum(axis=0)
    to_all = jnp.broadcast_to(jnp.concatenate([direct[1:, :, :128], direct[1:, :, 128:]], axis=0)[None], (Z, 6, 16, 128))
    mixed = jnp.concatenate(
        [to_all.reshape(Z, 96, 128), pairs[:, :3].reshape(Z, 48, 128), fours.reshape(Z, 24, 128)], axis=1
    )
    mixed = exchange(mixed, "z")
    m4 = mix(part4, direct[0], "yl", other4)
    own = mixed[:, :96]
    other = partner(own, "c")
    g34, g24, g14 = [
        jnp.concatenate([both_cores(own, other, 16 * n, 16), both_cores(own, other, 48 + 16 * n, 16)], axis=1)
        for n in range(3)
    ]
    sums = mixed[:, 96:].sum(axis=0)
    own = spread(jnp.concatenate([sums[16:48], sums[64:72]], axis=0), "z", Z)
    t = in_lanes(sums[0:16]) - times(m4, g34)
    got = partner(t, "yl")
    t = t + got
    m3 = mix(part3, t, "yh")
    t2 = in_rows(in_lanes(sums[48:56])) - times(m4, g24)
    t1 = in_rows(in_lanes(sums[56:64])) - times(m4, g14)
    other = partner(own, "c")
    g23, g13 = both_cores(own, other, 0, 16), both_cores(own, other, 16, 16)
    quarter = jnp.concatenate([own[:, 32:], other[:, 32:]], axis=0)
    half = ordered(at["yl"], quarter, partner(quarter, "yl"), 2)
    full = ordered(at["yh"], half, partner(half, "yh"), 1)
    g12 = ordered(core, full[:Z].reshape(128, 256), full[Z:].reshape(128, 256), 0)
    t = jnp.stack([t2 - in_lanes(times(m3, g23)), t1 - in_lanes(times(m3, g13))])
    t = t + partner(t, "yl")
    t = t + partner(t, "yh")
    m2 = mix(part2, t[0], "xl")
    t = t[1] - times(m2, g12)
    t = t + partner(t, "xl")
    m1 = mix(part1, t, "xh")

    last = spread(jnp.stack([m4, m3, m2, m1]), "z", Z)
    return finish(core, left_basis, x0, last, partner(last, "c"))


def solution(mesh):
    fine = Mesh(mesh.devices.reshape(SIZES), AXES)
    row = P(AXES, None)
    level = P(None, AXES, None)
    return jax.shard_map(
        local,
        mesh=fine,
        in_specs=(row, row, level, level, row, row, row, row),
        out_specs=row,
        check_vma=False,
    )
```

```python
import jax
import jax.numpy as jnp
from jax import lax
from jax.experimental import pallas as pl
from jax.experimental.pallas import tpu as pltpu
from jax.sharding import Mesh, PartitionSpec as P

AXES = ("xh", "xl", "yh", "yl", "z", "c")
SIZES = (2, 2, 2, 2, 8, 2)
Z = 8
STEPS = 4
F32 = jnp.float32
BF16 = jnp.bfloat16
PAIRS = ((3, 4), (2, 4), (1, 4), (2, 3), (1, 3), (1, 2))
DIRECT = (4, (3, 4), (2, 4), (1, 4))
SHARED = (3, (2, 3), (1, 3), 2, 1, (1, 2))


def dot(a, b, dims):
    return lax.dot_general(a, b, ((dims[0], dims[1]), ((), ())), preferred_element_type=F32)


def fdot(a, b, dims):
    return lax.dot_general(
        a, b, ((dims[0], dims[1]), ((), ())), precision=lax.Precision.HIGH, preferred_element_type=F32
    )


def pack_kernel(a_ref, b_ref, c_ref, d_ref, out_ref):
    for z in range(Z):
        out_ref[z, 0:16, :] = a_ref[...]
        out_ref[z, 16:24, :] = b_ref[...]
        out_ref[z, 24:28, :] = c_ref[...]
        out_ref[z, 28:30, :] = d_ref[...]
        out_ref[z, 30:32, :] = jnp.zeros((2, 512), F32)


def pack(k4, k3, k2, k1):
    return pl.pallas_call(pack_kernel, out_shape=jax.ShapeDtypeStruct((Z, 32, 512), F32), name="pack")(k4, k3, k2, k1)


def leaf_kernel(
    core_ref, pair_ref, inv_hbm, rhs_hbm, v_hbm, w_hbm, x_ref, keep_ref, give_ref, keep_shared_ref, give_shared_ref,
    inv_ref, rhs_ref, v_ref, w_ref, high_ref, low_ref, sems,
):
    rows = 1024 // STEPS
    count = [0]

    def load(src, dst):
        copy = pltpu.make_async_copy(src, dst, sems.at[count[0]])
        count[0] += 1
        copy.start()
        return copy

    wait_w, wait_v = {}, {}
    wait_w[4] = load(w_hbm.at[3], w_ref.at[2])
    wait_v[3] = load(v_hbm.at[2], v_ref.at[2])
    wait_v[2] = load(v_hbm.at[1], v_ref.at[1])
    wait_v[1] = load(v_hbm.at[0], v_ref.at[0])
    wait_w[3] = load(w_hbm.at[2], w_ref.at[1])
    wait_w[2] = load(w_hbm.at[1], w_ref.at[0])
    wait_rhs = load(rhs_hbm, rhs_ref)
    parts = [pl.ds(step * rows, rows) for step in range(STEPS)]
    wait_inv = [load(inv_hbm.at[part], inv_ref.at[part]) for part in parts]
    wait_v[4] = load(v_hbm.at[3], v_ref.at[3])
    first_core = core_ref[0] == 0
    first_lanes = pair_ref[0] == 0

    def store(name, value):
        low, high = value[:128], value[128:]
        keep = jnp.where(first_core, low, high).reshape(Z, 16, 256)
        give = jnp.where(first_core, high, low).reshape(Z, 16, 256)
        if name in DIRECT:
            keep_ref[:, DIRECT.index(name)] = keep
            give_ref[:, DIRECT.index(name)] = give
            return
        n = SHARED.index(name)
        for value, ref in ((keep, keep_shared_ref), (give, give_shared_ref)):
            left, right = value[:, :, :128], value[:, :, 128:]
            ref[0, :, n] = jnp.where(first_lanes, left, right)
            ref[1, :, n] = jnp.where(first_lanes, right, left)

    done = set()

    def ready(waits, level):
        if (id(waits), level) not in done:
            done.add((id(waits), level))
            waits[level].wait()

    turned = {}
    for j, k in PAIRS:
        ready(wait_w, k)
        if k not in turned:
            turned[k] = w_ref[k - 2].T
        ready(wait_v, j)
        store((j, k), dot(turned[k], v_ref[j - 1], ((1,), (0,))))
    wait_rhs.wait()
    rhs = rhs_ref[...]
    rhs_turned = rhs.T
    for step, part in enumerate(parts):
        wait_inv[step].wait()
        inv = inv_ref[part, :]
        x_ref[part, :] = jnp.dot(inv, rhs, preferred_element_type=F32)
        xt = dot(rhs_turned, inv, ((1,), (1,)))
        high = xt.astype(BF16)
        high_ref[:, part] = high
        low_ref[:, part] = (xt - high.astype(F32)).astype(BF16)
    for j in (4, 3, 2, 1):
        ready(wait_v, j)
        v = v_ref[j - 1]
        store(j, dot(high_ref[...], v, ((1,), (0,))) + dot(low_ref[...], v, ((1,), (0,))))


def leaf(core, pair, leaf_inv, right_side, right_basis, left_basis):
    any_space = pl.BlockSpec(memory_space=pl.ANY)
    return pl.pallas_call(
        leaf_kernel,
        in_specs=[pl.BlockSpec(memory_space=pltpu.SMEM)] * 2 + [any_space] * 4,
        out_shape=[
            jax.ShapeDtypeStruct((1024, 256), F32),
            jax.ShapeDtypeStruct((Z, 4, 16, 256), F32),
            jax.ShapeDtypeStruct((Z, 4, 16, 256), F32),
            jax.ShapeDtypeStruct((2, Z, 6, 16, 128), F32),
            jax.ShapeDtypeStruct((2, Z, 6, 16, 128), F32),
        ],
        scratch_shapes=[
            pltpu.VMEM((1024, 1024), BF16),
            pltpu.VMEM((1024, 256), BF16),
            pltpu.VMEM((4, 1024, 256), BF16),
            pltpu.VMEM((3, 1024, 256), BF16),
            pltpu.VMEM((256, 1024), BF16),
            pltpu.VMEM((256, 1024), BF16),
            pltpu.SemaphoreType.DMA((8 + STEPS,)),
        ],
        name="leaf",
    )(core.reshape(1), pair.reshape(1), leaf_inv, right_side, right_basis, left_basis)


def assemble_kernel(
    core_ref, yl_ref, yh_ref, xl_ref, rows, rows_c, a, a_c, b, b_c, e, e_c, k4_ref, k3_ref, k2_ref, k1_ref
):
    first = core_ref[0] == 0
    yl, yh, xl = yl_ref[0], yh_ref[0], xl_ref[0]
    near, far = jnp.where(yl == 0, 0, 1), jnp.where(yl == 0, 1, 0)
    up, down = jnp.where(yh == 0, 0, 2), jnp.where(yh == 0, 2, 0)
    left, right = jnp.where(xl == 0, 0, 4), jnp.where(xl == 0, 4, 0)

    def pair(own, other):
        return jnp.where(first, own, other), jnp.where(first, other, own)

    def both(own, other):
        return jnp.concatenate(pair(own, other), axis=0)

    for z in range(Z):
        low, high = pair(rows[z, 0:16], rows_c[z, 0:16])
        k4_ref[32 * z : 32 * z + 16] = low
        k4_ref[32 * z + 16 : 32 * z + 32] = high
        for t, own, other in ((near, rows[z, 16:24], rows_c[z, 16:24]), (far, a[z, 0:8], a_c[z, 0:8])):
            k3_ref[pl.ds(pl.multiple_of(128 * t + 16 * z, 16), 16)] = both(own, other)
        for t, own, other in (
            (up + near, rows[z, 24:28], rows_c[z, 24:28]),
            (up + far, a[z, 8:12], a_c[z, 8:12]),
            (down + near, b[z, 0:4], b_c[z, 0:4]),
            (down + far, b[z, 8:12], b_c[z, 8:12]),
        ):
            k2_ref[pl.ds(pl.multiple_of(64 * t + 8 * z, 8), 8)] = both(own, other)
    for z in range(0, Z, 2):
        for t, (own, other, row) in (
            (left + up + near, (rows, rows_c, 28)),
            (left + up + far, (a, a_c, 12)),
            (left + down + near, (b, b_c, 4)),
            (left + down + far, (b, b_c, 12)),
            (right + up + near, (e, e_c, 0)),
            (right + up + far, (e, e_c, 2)),
            (right + down + near, (e, e_c, 4)),
            (right + down + far, (e, e_c, 6)),
        ):
            tile = [both(own[y, row : row + 2], other[y, row : row + 2]) for y in (z, z + 1)]
            k1_ref[pl.ds(pl.multiple_of(32 * t + 4 * z, 8), 8)] = jnp.concatenate(tile, axis=0)


def assemble(at, pieces):
    scalars = [at[axis].reshape(1) for axis in ("c", "yl", "yh", "xl")]
    return pl.pallas_call(
        assemble_kernel,
        in_specs=[pl.BlockSpec(memory_space=pltpu.SMEM)] * 4 + [pl.BlockSpec()] * len(pieces),
        out_shape=[jax.ShapeDtypeStruct((256, 512), F32)] * 4,
        name="assemble",
    )(*scalars, *pieces)


def partner(block, axis):
    return lax.ppermute(block, axis, [(0, 1), (1, 0)])


def ordered(bit, own, other, axis):
    low = jnp.where(bit == 0, own, other)
    high = jnp.where(bit == 0, other, own)
    return jnp.concatenate([low, high], axis=axis)


def exchange(block, axes):
    return lax.all_to_all(block, axes, 0, 0, tiled=True)


def spread(block, axes, count):
    return exchange(jnp.broadcast_to(block[None], (count,) + block.shape), axes)


def local(right_side, leaf_inv, right_basis, left_basis, k1, k2, k3, k4):
    at = {axis: lax.axis_index(axis) for axis in AXES}
    core = at["c"]
    rows = exchange(pack(k4, k3, k2, k1), "z")
    x0, keep, give, keep_shared, give_shared = leaf(
        core, at["yl"], leaf_inv, right_side, right_basis, left_basis
    )
    mine = keep + partner(give, "c")
    got_shared = partner(give_shared, "c")
    got = partner(keep_shared[1] + got_shared[1], "yl")
    direct = exchange(mine, "z")
    pairs = (keep_shared[0] + got_shared[0]) + got
    upper = at["yh"] == 0
    fours = pairs[:, 3:5]
    give = jnp.where(upper, fours[:, :, 8:], fours[:, :, :8]).reshape(Z, 1, 16, 128)
    got = partner(jnp.concatenate([give, pairs[:, 5:]], axis=1), "yh")
    keep = jnp.where(upper, fours[:, :, :8], fours[:, :, 8:]).reshape(Z, 1, 16, 128)
    fours = jnp.concatenate([keep, pairs[:, 5:]], axis=1) + got
    fours, rows = lax.optimization_barrier((fours, rows))
    a0 = rows[:, 16:32]
    a1 = partner(a0, "yl")
    b0 = jnp.concatenate([a0[:, 8:], a1[:, 8:]], axis=1)
    b1 = partner(b0, "yh")
    e0 = jnp.concatenate([b0[:, 4:6], b0[:, 12:14], b1[:, 4:6], b1[:, 12:14]], axis=1)
    e1 = partner(e0, "xl")
    pieces = [piece for own in (rows, a1, b1, e1) for piece in (own, partner(own, "c"))]
    reduced = assemble(at, pieces)

    def both_cores(own, other, first, count):
        own = own[:, first : first + count].reshape(Z * count, -1)
        other = other[:, first : first + count].reshape(Z * count, -1)
        return ordered(core, own, other, 0)

    def mix(k, own, axis):
        stack = ordered(at[axis], own, partner(own, axis), 1)
        return fdot(stack, k, ((1,), (1,)))

    def times(m, g):
        return fdot(m, g, ((1,), (0,)))

    def in_lanes(block):
        zero = jnp.zeros_like(block)
        first = at["yl"] == 0
        return jnp.concatenate([jnp.where(first, block, zero), jnp.where(first, zero, block)], axis=1)

    def in_rows(block):
        zero = jnp.zeros_like(block)
        return jnp.concatenate([jnp.where(upper, block, zero), jnp.where(upper, zero, block)], axis=0)

    direct = direct.sum(axis=0)
    to_all = jnp.broadcast_to(jnp.concatenate([direct[1:, :, :128], direct[1:, :, 128:]], axis=0)[None], (Z, 6, 16, 128))
    mixed = jnp.concatenate(
        [to_all.reshape(Z, 96, 128), pairs[:, :3].reshape(Z, 48, 128), fours.reshape(Z, 32, 128)], axis=1
    )
    mixed = exchange(mixed, "z")
    m4 = mix(reduced[0], direct[0], "yl")
    own = mixed[:, :96]
    other = partner(own, "c")
    g34, g24, g14 = [
        jnp.concatenate([both_cores(own, other, 16 * n, 16), both_cores(own, other, 48 + 16 * n, 16)], axis=1)
        for n in range(3)
    ]
    sums = mixed[:, 96:].sum(axis=0)
    third = spread(jnp.concatenate([sums[16:48], sums[64:80]], axis=0), "z", Z)
    t = in_lanes(sums[0:16]) - times(m4, g34)
    got = partner(t, "yl")
    t = t + got
    m3 = mix(reduced[1], t, "yh")
    own, m3 = lax.optimization_barrier((third, m3))
    t2 = in_rows(in_lanes(sums[48:56])) - times(m4, g24)
    t1 = in_rows(in_lanes(sums[56:64])) - times(m4, g14)
    other = partner(own, "c")
    g23, g13 = both_cores(own, other, 0, 16), both_cores(own, other, 16, 16)
    half = both_cores(own, other, 32, 16)
    g12 = ordered(at["yl"], half, partner(half, "yl"), 1)
    t = jnp.stack([t2 - in_lanes(times(m3, g23)), t1 - in_lanes(times(m3, g13))])
    t = t + partner(t, "yl")
    t = t + partner(t, "yh")
    m2 = mix(reduced[2], t[0], "xl")
    t = t[1] - times(m2, g12)
    t = t + partner(t, "xl")
    m1 = mix(reduced[3], t, "xh")

    own = spread(jnp.concatenate([m4, m3, m2, m1], axis=0), "z", Z)
    other = partner(own, "c")
    out = x0
    for n, level in enumerate((4, 3, 2, 1)):
        m = both_cores(own, other, 16 * n, 16)
        high = lax.reduce_precision(m, 8, 7)
        low = (m - high).astype(BF16)
        high = high.astype(BF16)
        left = left_basis[level - 1]
        out = out - (dot(left, high, ((1,), (1,))) + dot(left, low, ((1,), (1,))))
    return out


def solution(mesh):
    fine = Mesh(mesh.devices.reshape(SIZES), AXES)
    row = P(AXES, None)
    level = P(None, AXES, None)
    return jax.shard_map(
        local,
        mesh=fine,
        in_specs=(row, row, level, level, row, row, row, row),
        out_specs=row,
        check_vma=False,
    )
```

```python
import jax
import jax.numpy as jnp
from jax import lax
from jax.experimental import pallas as pl
from jax.experimental.pallas import tpu as pltpu
from jax.sharding import Mesh, PartitionSpec as P

AXES = ("xh", "xl", "yh", "yl", "z", "c")
SIZES = (2, 2, 2, 2, 8, 2)
Z = 8
STEPS = 4
F32 = jnp.float32
BF16 = jnp.bfloat16
PAIRS = ((3, 4), (2, 4), (1, 4), (2, 3), (1, 3), (1, 2))
DIRECT = (4, (3, 4), (2, 4), (1, 4))
SHARED = (3, (2, 3), (1, 3), 2, 1, (1, 2))


def dot(a, b, dims):
    return lax.dot_general(a, b, ((dims[0], dims[1]), ((), ())), preferred_element_type=F32)


def fdot(a, b, dims):
    return lax.dot_general(
        a, b, ((dims[0], dims[1]), ((), ())), precision=lax.Precision.HIGH, preferred_element_type=F32
    )


def pack_kernel(a_ref, b_ref, c_ref, d_ref, out_ref):
    for z in range(Z):
        out_ref[z, 0:16, :] = a_ref[...]
        out_ref[z, 16:24, :] = b_ref[...]
        out_ref[z, 24:28, :] = c_ref[...]
        out_ref[z, 28:30, :] = d_ref[...]
        out_ref[z, 30:32, :] = jnp.zeros((2, 512), F32)


def pack(k4, k3, k2, k1):
    return pl.pallas_call(pack_kernel, out_shape=jax.ShapeDtypeStruct((Z, 32, 512), F32), name="pack")(k4, k3, k2, k1)


def leaf_kernel(
    core_ref, pair_ref, inv_hbm, rhs_hbm, v_hbm, w_hbm, x_ref, keep_ref, give_ref, keep_shared_ref, give_shared_ref,
    inv_ref, rhs_ref, v_ref, w_ref, high_ref, low_ref, sems,
):
    rows = 1024 // STEPS
    count = [0]

    def load(src, dst):
        copy = pltpu.make_async_copy(src, dst, sems.at[count[0]])
        count[0] += 1
        copy.start()
        return copy

    wait_w, wait_v = {}, {}
    wait_w[4] = load(w_hbm.at[3], w_ref.at[2])
    wait_v[3] = load(v_hbm.at[2], v_ref.at[2])
    wait_v[2] = load(v_hbm.at[1], v_ref.at[1])
    wait_v[1] = load(v_hbm.at[0], v_ref.at[0])
    wait_w[3] = load(w_hbm.at[2], w_ref.at[1])
    wait_w[2] = load(w_hbm.at[1], w_ref.at[0])
    wait_rhs = load(rhs_hbm, rhs_ref)
    parts = [pl.ds(step * rows, rows) for step in range(STEPS)]
    wait_inv = [load(inv_hbm.at[part], inv_ref.at[part]) for part in parts]
    wait_v[4] = load(v_hbm.at[3], v_ref.at[3])
    first_core = core_ref[0] == 0
    first_lanes = pair_ref[0] == 0

    def store(name, value):
        low, high = value[:128], value[128:]
        keep = jnp.where(first_core, low, high).reshape(Z, 16, 256)
        give = jnp.where(first_core, high, low).reshape(Z, 16, 256)
        if name in DIRECT:
            keep_ref[:, DIRECT.index(name)] = keep
            give_ref[:, DIRECT.index(name)] = give
            return
        n = SHARED.index(name)
        for value, ref in ((keep, keep_shared_ref), (give, give_shared_ref)):
            left, right = value[:, :, :128], value[:, :, 128:]
            ref[0, :, n] = jnp.where(first_lanes, left, right)
            ref[1, :, n] = jnp.where(first_lanes, right, left)

    done = set()

    def ready(waits, level):
        if (id(waits), level) not in done:
            done.add((id(waits), level))
            waits[level].wait()

    turned = {}
    for j, k in PAIRS:
        ready(wait_w, k)
        if k not in turned:
            turned[k] = w_ref[k - 2].T
        ready(wait_v, j)
        store((j, k), dot(turned[k], v_ref[j - 1], ((1,), (0,))))
    wait_rhs.wait()
    rhs = rhs_ref[...]
    rhs_turned = rhs.T
    for step, part in enumerate(parts):
        wait_inv[step].wait()
        inv = inv_ref[part, :]
        x_ref[part, :] = jnp.dot(inv, rhs, preferred_element_type=F32)
        xt = dot(rhs_turned, inv, ((1,), (1,)))
        high = xt.astype(BF16)
        high_ref[:, part] = high
        low_ref[:, part] = (xt - high.astype(F32)).astype(BF16)
    for j in (4, 3, 2, 1):
        ready(wait_v, j)
        v = v_ref[j - 1]
        store(j, dot(high_ref[...], v, ((1,), (0,))) + dot(low_ref[...], v, ((1,), (0,))))


def leaf(core, pair, leaf_inv, right_side, right_basis, left_basis):
    any_space = pl.BlockSpec(memory_space=pl.ANY)
    return pl.pallas_call(
        leaf_kernel,
        in_specs=[pl.BlockSpec(memory_space=pltpu.SMEM)] * 2 + [any_space] * 4,
        out_shape=[
            jax.ShapeDtypeStruct((1024, 256), F32),
            jax.ShapeDtypeStruct((Z, 4, 16, 256), F32),
            jax.ShapeDtypeStruct((Z, 4, 16, 256), F32),
            jax.ShapeDtypeStruct((2, Z, 6, 16, 128), F32),
            jax.ShapeDtypeStruct((2, Z, 6, 16, 128), F32),
        ],
        scratch_shapes=[
            pltpu.VMEM((1024, 1024), BF16),
            pltpu.VMEM((1024, 256), BF16),
            pltpu.VMEM((4, 1024, 256), BF16),
            pltpu.VMEM((3, 1024, 256), BF16),
            pltpu.VMEM((256, 1024), BF16),
            pltpu.VMEM((256, 1024), BF16),
            pltpu.SemaphoreType.DMA((8 + STEPS,)),
        ],
        name="leaf",
    )(core.reshape(1), pair.reshape(1), leaf_inv, right_side, right_basis, left_basis)


def offsets(bit, step):
    return jnp.where(bit == 0, 0, step), jnp.where(bit == 0, step, 0)


def pair(core_ref, own, other):
    first = core_ref[0] == 0
    return jnp.where(first, own, other), jnp.where(first, other, own)


def fine_kernel(core_ref, yl_ref, rows, rows_c, a, a_c, k4_ref, k3_ref):
    near, far = offsets(yl_ref[0], 1)
    for z in range(Z):
        low, high = pair(core_ref, rows[z, 0:16], rows_c[z, 0:16])
        k4_ref[32 * z : 32 * z + 16] = low
        k4_ref[32 * z + 16 : 32 * z + 32] = high
        for t, own, other in ((near, rows[z, 16:24], rows_c[z, 16:24]), (far, a[z, 0:8], a_c[z, 0:8])):
            both = jnp.concatenate(pair(core_ref, own, other), axis=0)
            k3_ref[pl.ds(pl.multiple_of(128 * t + 16 * z, 16), 16)] = both


def coarse_kernel(core_ref, yl_ref, yh_ref, xl_ref, rows, rows_c, a, a_c, b, b_c, e, e_c, k2_ref, k1_ref):
    near, far = offsets(yl_ref[0], 1)
    up, down = offsets(yh_ref[0], 2)
    left, right = offsets(xl_ref[0], 4)

    def both(own, other):
        return jnp.concatenate(pair(core_ref, own, other), axis=0)

    for z in range(Z):
        for t, own, other in (
            (up + near, rows[z, 24:28], rows_c[z, 24:28]),
            (up + far, a[z, 8:12], a_c[z, 8:12]),
            (down + near, b[z, 0:4], b_c[z, 0:4]),
            (down + far, b[z, 8:12], b_c[z, 8:12]),
        ):
            k2_ref[pl.ds(pl.multiple_of(64 * t + 8 * z, 8), 8)] = both(own, other)
    for z in range(0, Z, 2):
        for t, (own, other, row) in (
            (left + up + near, (rows, rows_c, 28)),
            (left + up + far, (a, a_c, 12)),
            (left + down + near, (b, b_c, 4)),
            (left + down + far, (b, b_c, 12)),
            (right + up + near, (e, e_c, 0)),
            (right + up + far, (e, e_c, 2)),
            (right + down + near, (e, e_c, 4)),
            (right + down + far, (e, e_c, 6)),
        ):
            tile = [both(own[y, row : row + 2], other[y, row : row + 2]) for y in (z, z + 1)]
            k1_ref[pl.ds(pl.multiple_of(32 * t + 4 * z, 8), 8)] = jnp.concatenate(tile, axis=0)


def assemble(kernel, scalars, pieces):
    return pl.pallas_call(
        kernel,
        in_specs=[pl.BlockSpec(memory_space=pltpu.SMEM)] * len(scalars) + [pl.BlockSpec()] * len(pieces),
        out_shape=[jax.ShapeDtypeStruct((256, 512), F32)] * 2,
    )(*[scalar.reshape(1) for scalar in scalars], *pieces)


def partner(block, axis):
    return lax.ppermute(block, axis, [(0, 1), (1, 0)])


def ordered(bit, own, other, axis):
    low = jnp.where(bit == 0, own, other)
    high = jnp.where(bit == 0, other, own)
    return jnp.concatenate([low, high], axis=axis)


def exchange(block, axes):
    return lax.all_to_all(block, axes, 0, 0, tiled=True)


def spread(block, axes, count):
    return exchange(jnp.broadcast_to(block[None], (count,) + block.shape), axes)


def local(right_side, leaf_inv, right_basis, left_basis, k1, k2, k3, k4):
    at = {axis: lax.axis_index(axis) for axis in AXES}
    core = at["c"]
    rows = exchange(pack(k4, k3, k2, k1), "z")
    x0, keep, give, keep_shared, give_shared = leaf(
        core, at["yl"], leaf_inv, right_side, right_basis, left_basis
    )
    mine = keep + partner(give, "c")
    got_shared = partner(give_shared, "c")
    got = partner(keep_shared[1] + got_shared[1], "yl")
    direct = exchange(mine, "z")
    pairs = (keep_shared[0] + got_shared[0]) + got
    upper = at["yh"] == 0
    fours = pairs[:, 3:5]
    give = jnp.where(upper, fours[:, :, 8:], fours[:, :, :8]).reshape(Z, 1, 16, 128)
    got = partner(jnp.concatenate([give, pairs[:, 5:]], axis=1), "yh")
    keep = jnp.where(upper, fours[:, :, :8], fours[:, :, 8:]).reshape(Z, 1, 16, 128)
    fours = jnp.concatenate([keep, pairs[:, 5:]], axis=1) + got
    fours, rows = lax.optimization_barrier((fours, rows))
    rows_c = partner(rows, "c")
    a0 = rows[:, 16:32]
    a1 = partner(a0, "yl")
    a1_c = partner(a1, "c")
    b0 = jnp.concatenate([a0[:, 8:], a1[:, 8:]], axis=1)
    b1 = partner(b0, "yh")
    b1_c = partner(b1, "c")
    e0 = jnp.concatenate([b0[:, 4:6], b0[:, 12:14], b1[:, 4:6], b1[:, 12:14]], axis=1)
    e1 = partner(e0, "xl")
    e1_c = partner(e1, "c")
    pieces = [rows, rows_c, a1, a1_c]
    full4, full3 = assemble(fine_kernel, [core, at["yl"]], pieces)
    scalars = [at[axis] for axis in ("c", "yl", "yh", "xl")]
    full2, full1 = assemble(coarse_kernel, scalars, pieces + [b1, b1_c, e1, e1_c])

    def both_cores(own, other, first, count):
        own = own[:, first : first + count].reshape(Z * count, -1)
        other = other[:, first : first + count].reshape(Z * count, -1)
        return ordered(core, own, other, 0)

    def mix(k, own, other, axis):
        return fdot(ordered(at[axis], own, other, 1), k, ((1,), (1,)))

    def of_four(block, axes):
        return [block] + [lax.ppermute(block, axes, [(i, i ^ k) for i in range(4)]) for k in (1, 2, 3)]

    def times(m, g):
        return fdot(m, g, ((1,), (0,)))

    def in_lanes(block):
        zero = jnp.zeros_like(block)
        first = at["yl"] == 0
        return jnp.concatenate([jnp.where(first, block, zero), jnp.where(first, zero, block)], axis=1)

    def in_rows(block):
        zero = jnp.zeros_like(block)
        return jnp.concatenate([jnp.where(upper, block, zero), jnp.where(upper, zero, block)], axis=0)

    direct = direct.sum(axis=0)
    to_all = jnp.broadcast_to(jnp.concatenate([direct[1:, :, :128], direct[1:, :, 128:]], axis=0)[None], (Z, 6, 16, 128))
    mixed = jnp.concatenate(
        [to_all.reshape(Z, 96, 128), pairs[:, :3].reshape(Z, 48, 128), fours.reshape(Z, 32, 128)], axis=1
    )
    mixed = exchange(mixed, "z")
    m4 = mix(full4, direct[0], partner(direct[0], "yl"), "yl")
    own = mixed[:, :96]
    other = partner(own, "c")
    g34, g24, g14 = [
        jnp.concatenate([both_cores(own, other, 16 * n, 16), both_cores(own, other, 48 + 16 * n, 16)], axis=1)
        for n in range(3)
    ]
    sums = mixed[:, 96:].sum(axis=0)
    third = spread(jnp.concatenate([sums[16:48], sums[64:80]], axis=0), "z", Z)
    t = in_lanes(sums[0:16]) - times(m4, g34)
    got = partner(t, "yl")
    t = t + got
    m3 = mix(full3, t, partner(t, "yh"), "yh")
    own, m3 = lax.optimization_barrier((third, m3))
    t2 = in_rows(in_lanes(sums[48:56])) - times(m4, g24)
    t1 = in_rows(in_lanes(sums[56:64])) - times(m4, g14)
    other = partner(own, "c")
    g23, g13 = both_cores(own, other, 0, 16), both_cores(own, other, 16, 16)
    half = both_cores(own, other, 32, 16)
    g12 = ordered(at["yl"], half, partner(half, "yl"), 1)
    t = jnp.stack([t2 - in_lanes(times(m3, g23)), t1 - in_lanes(times(m3, g13))])
    t = sum(of_four(t, ("yh", "yl")))
    m2 = mix(full2, t[0], partner(t[0], "xl"), "xl")
    four = of_four(t[1] - times(m2, g12), ("xh", "xl"))
    m1 = mix(full1, four[0] + four[1], four[2] + four[3], "xh")

    own = spread(jnp.concatenate([m4, m3, m2, m1], axis=0), "z", Z)
    other = partner(own, "c")
    m = jnp.stack([both_cores(own, other, 16 * n, 16) for n in (3, 2, 1, 0)])
    high = lax.reduce_precision(m, 8, 7)
    low = (m - high).astype(BF16)
    dims = ((0, 2), (0, 2))
    return x0 - (dot(left_basis, high.astype(BF16), dims) + dot(left_basis, low, dims))


def solution(mesh):
    fine = Mesh(mesh.devices.reshape(SIZES), AXES)
    row = P(AXES, None)
    level = P(None, AXES, None)
    return jax.shard_map(
        local,
        mesh=fine,
        in_specs=(row, row, level, level, row, row, row, row),
        out_specs=row,
        check_vma=False,
    )
```

```python
import jax
import jax.numpy as jnp
from jax import lax
from jax.experimental import pallas as pl
from jax.experimental.pallas import tpu as pltpu
from jax.sharding import Mesh, PartitionSpec as P

AXES = ("xh", "xl", "yh", "yl", "z", "c")
SIZES = (2, 2, 2, 2, 8, 2)
Z = 8
STEPS = 4
F32 = jnp.float32
BF16 = jnp.bfloat16
PAIRS = ((3, 4), (2, 4), (1, 4), (2, 3), (1, 3), (1, 2))
DIRECT = (4, (3, 4), (2, 4), (1, 4))
SHARED = (3, (2, 3), (1, 3), 2, 1, (1, 2))


def dot(a, b, dims):
    return lax.dot_general(a, b, ((dims[0], dims[1]), ((), ())), preferred_element_type=F32)


def fdot(a, b, dims):
    return lax.dot_general(
        a, b, ((dims[0], dims[1]), ((), ())), precision=lax.Precision.HIGH, preferred_element_type=F32
    )


def pack_kernel(a_ref, b_ref, c_ref, d_ref, out_ref):
    for z in range(Z):
        out_ref[z, 0:16, :] = a_ref[...]
        out_ref[z, 16:24, :] = b_ref[...]
        out_ref[z, 24:28, :] = c_ref[...]
        out_ref[z, 28:30, :] = d_ref[...]
        out_ref[z, 30:32, :] = jnp.zeros((2, 512), F32)


def pack(k4, k3, k2, k1):
    return pl.pallas_call(pack_kernel, out_shape=jax.ShapeDtypeStruct((Z, 32, 512), F32), name="pack")(k4, k3, k2, k1)


def leaf_kernel(
    core_ref, pair_ref, inv_hbm, rhs_hbm, v_hbm, w_hbm, x_ref, keep_ref, give_ref, keep_shared_ref, give_shared_ref,
    inv_ref, rhs_ref, v_ref, w_ref, high_ref, low_ref, sems,
):
    rows = 1024 // STEPS
    count = [0]

    def load(src, dst):
        copy = pltpu.make_async_copy(src, dst, sems.at[count[0]])
        count[0] += 1
        copy.start()
        return copy

    wait_w, wait_v = {}, {}
    wait_w[4] = load(w_hbm.at[3], w_ref.at[2])
    wait_v[3] = load(v_hbm.at[2], v_ref.at[2])
    wait_v[2] = load(v_hbm.at[1], v_ref.at[1])
    wait_v[1] = load(v_hbm.at[0], v_ref.at[0])
    wait_w[3] = load(w_hbm.at[2], w_ref.at[1])
    wait_w[2] = load(w_hbm.at[1], w_ref.at[0])
    wait_rhs = load(rhs_hbm, rhs_ref)
    parts = [pl.ds(step * rows, rows) for step in range(STEPS)]
    wait_inv = [load(inv_hbm.at[part], inv_ref.at[part]) for part in parts]
    wait_v[4] = load(v_hbm.at[3], v_ref.at[3])
    first_core = core_ref[0] == 0
    first_lanes = pair_ref[0] == 0

    def store(name, value):
        low, high = value[:128], value[128:]
        keep = jnp.where(first_core, low, high).reshape(Z, 16, 256)
        give = jnp.where(first_core, high, low).reshape(Z, 16, 256)
        if name in DIRECT:
            keep_ref[:, DIRECT.index(name)] = keep
            give_ref[:, DIRECT.index(name)] = give
            return
        n = SHARED.index(name)
        for value, ref in ((keep, keep_shared_ref), (give, give_shared_ref)):
            left, right = value[:, :, :128], value[:, :, 128:]
            ref[0, :, n] = jnp.where(first_lanes, left, right)
            ref[1, :, n] = jnp.where(first_lanes, right, left)

    done = set()

    def ready(waits, level):
        if (id(waits), level) not in done:
            done.add((id(waits), level))
            waits[level].wait()

    turned = {}
    for j, k in PAIRS:
        ready(wait_w, k)
        if k not in turned:
            turned[k] = w_ref[k - 2].T
        ready(wait_v, j)
        store((j, k), dot(turned[k], v_ref[j - 1], ((1,), (0,))))
    wait_rhs.wait()
    rhs = rhs_ref[...]
    rhs_turned = rhs.T
    for step, part in enumerate(parts):
        wait_inv[step].wait()
        inv = inv_ref[part, :]
        x_ref[part, :] = jnp.dot(inv, rhs, preferred_element_type=F32)
        xt = dot(rhs_turned, inv, ((1,), (1,)))
        high = xt.astype(BF16)
        high_ref[:, part] = high
        low_ref[:, part] = (xt - high.astype(F32)).astype(BF16)
    for j in (4, 3, 2, 1):
        ready(wait_v, j)
        v = v_ref[j - 1]
        store(j, dot(high_ref[...], v, ((1,), (0,))) + dot(low_ref[...], v, ((1,), (0,))))


def leaf(core, pair, leaf_inv, right_side, right_basis, left_basis):
    any_space = pl.BlockSpec(memory_space=pl.ANY)
    return pl.pallas_call(
        leaf_kernel,
        in_specs=[pl.BlockSpec(memory_space=pltpu.SMEM)] * 2 + [any_space] * 4,
        out_shape=[
            jax.ShapeDtypeStruct((1024, 256), F32),
            jax.ShapeDtypeStruct((Z, 4, 16, 256), F32),
            jax.ShapeDtypeStruct((Z, 4, 16, 256), F32),
            jax.ShapeDtypeStruct((2, Z, 6, 16, 128), F32),
            jax.ShapeDtypeStruct((2, Z, 6, 16, 128), F32),
        ],
        scratch_shapes=[
            pltpu.VMEM((1024, 1024), BF16),
            pltpu.VMEM((1024, 256), BF16),
            pltpu.VMEM((4, 1024, 256), BF16),
            pltpu.VMEM((3, 1024, 256), BF16),
            pltpu.VMEM((256, 1024), BF16),
            pltpu.VMEM((256, 1024), BF16),
            pltpu.SemaphoreType.DMA((8 + STEPS,)),
        ],
        name="leaf",
    )(core.reshape(1), pair.reshape(1), leaf_inv, right_side, right_basis, left_basis)


def offsets(bit, step):
    return jnp.where(bit == 0, 0, step), jnp.where(bit == 0, step, 0)


def pair(core_ref, own, other):
    first = core_ref[0] == 0
    return jnp.where(first, own, other), jnp.where(first, other, own)


def fine_kernel(core_ref, yl_ref, rows, rows_c, a, a_c, k4_ref, k3_ref):
    near, far = offsets(yl_ref[0], 1)
    for z in range(Z):
        low, high = pair(core_ref, rows[z, 0:16], rows_c[z, 0:16])
        k4_ref[32 * z : 32 * z + 16] = low
        k4_ref[32 * z + 16 : 32 * z + 32] = high
        for t, own, other in ((near, rows[z, 16:24], rows_c[z, 16:24]), (far, a[z, 0:8], a_c[z, 0:8])):
            both = jnp.concatenate(pair(core_ref, own, other), axis=0)
            k3_ref[pl.ds(pl.multiple_of(128 * t + 16 * z, 16), 16)] = both


def coarse_kernel(core_ref, yl_ref, yh_ref, xl_ref, rows, rows_c, a, a_c, b, b_c, e, e_c, k2_ref, k1_ref):
    near, far = offsets(yl_ref[0], 1)
    up, down = offsets(yh_ref[0], 2)
    left, right = offsets(xl_ref[0], 4)

    def both(own, other):
        return jnp.concatenate(pair(core_ref, own, other), axis=0)

    for z in range(Z):
        for t, own, other in (
            (up + near, rows[z, 24:28], rows_c[z, 24:28]),
            (up + far, a[z, 8:12], a_c[z, 8:12]),
            (down + near, b[z, 0:4], b_c[z, 0:4]),
            (down + far, b[z, 8:12], b_c[z, 8:12]),
        ):
            k2_ref[pl.ds(pl.multiple_of(64 * t + 8 * z, 8), 8)] = both(own, other)
    for z in range(0, Z, 2):
        for t, (own, other, row) in (
            (left + up + near, (rows, rows_c, 28)),
            (left + up + far, (a, a_c, 12)),
            (left + down + near, (b, b_c, 4)),
            (left + down + far, (b, b_c, 12)),
            (right + up + near, (e, e_c, 0)),
            (right + up + far, (e, e_c, 2)),
            (right + down + near, (e, e_c, 4)),
            (right + down + far, (e, e_c, 6)),
        ):
            tile = [both(own[y, row : row + 2], other[y, row : row + 2]) for y in (z, z + 1)]
            k1_ref[pl.ds(pl.multiple_of(32 * t + 4 * z, 8), 8)] = jnp.concatenate(tile, axis=0)


def assemble(kernel, scalars, pieces):
    return pl.pallas_call(
        kernel,
        in_specs=[pl.BlockSpec(memory_space=pltpu.SMEM)] * len(scalars) + [pl.BlockSpec()] * len(pieces),
        out_shape=[jax.ShapeDtypeStruct((256, 512), F32)] * 2,
    )(*[scalar.reshape(1) for scalar in scalars], *pieces)


def partner(block, axis):
    return lax.ppermute(block, axis, [(0, 1), (1, 0)])


def ordered(bit, own, other, axis):
    low = jnp.where(bit == 0, own, other)
    high = jnp.where(bit == 0, other, own)
    return jnp.concatenate([low, high], axis=axis)


def exchange(block, axes):
    return lax.all_to_all(block, axes, 0, 0, tiled=True)


def spread(block, axes, count):
    return exchange(jnp.broadcast_to(block[None], (count,) + block.shape), axes)


def local(right_side, leaf_inv, right_basis, left_basis, k1, k2, k3, k4):
    at = {axis: lax.axis_index(axis) for axis in AXES}
    core = at["c"]
    rows = exchange(pack(k4, k3, k2, k1), "z")
    x0, keep, give, keep_shared, give_shared = leaf(
        core, at["yl"], leaf_inv, right_side, right_basis, left_basis
    )
    mine = partner(give, "c")
    mine = keep + mine
    got_shared = partner(give_shared, "c")
    got = partner(keep_shared[1] + got_shared[1], "yl")
    direct = exchange(mine, "z")
    pairs = (keep_shared[0] + got_shared[0]) + got
    pairs, rows = lax.optimization_barrier((pairs, rows))
    upper = at["yh"] == 0
    fours = pairs[:, 3:5]
    give = jnp.where(upper, fours[:, :, 8:], fours[:, :, :8]).reshape(Z, 1, 16, 128)
    got = partner(jnp.concatenate([give, pairs[:, 5:]], axis=1), "yh")
    keep = jnp.where(upper, fours[:, :, :8], fours[:, :, 8:]).reshape(Z, 1, 16, 128)
    fours = jnp.concatenate([keep, pairs[:, 5:]], axis=1) + got
    rows_c = partner(rows, "c")
    a0 = rows[:, 16:32]
    a1 = partner(a0, "yl")
    a1_c = partner(a1, "c")
    b0 = jnp.concatenate([a0[:, 8:], a1[:, 8:]], axis=1)
    b1 = partner(b0, "yh")
    b1_c = partner(b1, "c")
    e0 = jnp.concatenate([b0[:, 4:6], b0[:, 12:14], b1[:, 4:6], b1[:, 12:14]], axis=1)
    e1 = partner(e0, "xl")
    e1_c = partner(e1, "c")
    pieces = [rows, rows_c, a1, a1_c]
    full4, full3 = assemble(fine_kernel, [core, at["yl"]], pieces)
    scalars = [at[axis] for axis in ("c", "yl", "yh", "xl")]
    full2, full1 = assemble(coarse_kernel, scalars, pieces + [b1, b1_c, e1, e1_c])

    def both_cores(own, other, first, count):
        own = own[:, first : first + count].reshape(Z * count, -1)
        other = other[:, first : first + count].reshape(Z * count, -1)
        return ordered(core, own, other, 0)

    def mix(k, own, other, axis):
        return fdot(ordered(at[axis], own, other, 1), k, ((1,), (1,)))

    def of_four(block, axes):
        return [block] + [lax.ppermute(block, axes, [(i, i ^ k) for i in range(4)]) for k in (1, 2, 3)]

    def times(m, g):
        return fdot(m, g, ((1,), (0,)))

    def in_lanes(block):
        zero = jnp.zeros_like(block)
        first = at["yl"] == 0
        return jnp.concatenate([jnp.where(first, block, zero), jnp.where(first, zero, block)], axis=1)

    def in_rows(block):
        zero = jnp.zeros_like(block)
        return jnp.concatenate([jnp.where(upper, block, zero), jnp.where(upper, zero, block)], axis=0)

    direct = direct.sum(axis=0)
    to_all = jnp.broadcast_to(jnp.concatenate([direct[1:, :, :128], direct[1:, :, 128:]], axis=0)[None], (Z, 6, 16, 128))
    mixed = jnp.concatenate(
        [to_all.reshape(Z, 96, 128), pairs[:, :3].reshape(Z, 48, 128), fours.reshape(Z, 32, 128)], axis=1
    )
    mixed = exchange(mixed, "z")
    m4 = mix(full4, direct[0], partner(direct[0], "yl"), "yl")
    own = mixed[:, :96]
    other = partner(own, "c")
    g34, g24, g14 = [
        jnp.concatenate([both_cores(own, other, 16 * n, 16), both_cores(own, other, 48 + 16 * n, 16)], axis=1)
        for n in range(3)
    ]
    sums = mixed[:, 96:].sum(axis=0)
    third = spread(jnp.concatenate([sums[16:48], sums[64:80]], axis=0), "z", Z)
    t = in_lanes(sums[0:16]) - times(m4, g34)
    got = partner(t, "yl")
    t = t + got
    m3 = mix(full3, t, partner(t, "yh"), "yh")
    own, m3 = lax.optimization_barrier((third, m3))
    early = spread(jnp.concatenate([m4, m3], axis=0), "z", Z)
    t2 = in_rows(in_lanes(sums[48:56])) - times(m4, g24)
    t1 = in_rows(in_lanes(sums[56:64])) - times(m4, g14)
    other = partner(own, "c")
    g23, g13 = both_cores(own, other, 0, 16), both_cores(own, other, 16, 16)
    half = both_cores(own, other, 32, 16)
    g12 = ordered(at["yl"], half, partner(half, "yl"), 1)
    t = jnp.stack([t2 - in_lanes(times(m3, g23)), t1 - in_lanes(times(m3, g13))])
    four = of_four(t, ("yh", "yl"))
    t = (four[0] + four[1]) + (four[2] + four[3])
    m2 = mix(full2, t[0], partner(t[0], "xl"), "xl")
    four = of_four(t[1] - times(m2, g12), ("xh", "xl"))
    m1 = mix(full1, four[0] + four[1], four[2] + four[3], "xh")

    def correct(out, own, other, levels):
        m = jnp.stack([both_cores(own, other, row, 16) for row in (16, 0)])
        high = lax.reduce_precision(m, 8, 7)
        low = (m - high).astype(BF16)
        left, dims = left_basis[levels], ((0, 2), (0, 2))
        return out - (dot(left, high.astype(BF16), dims) + dot(left, low, dims))

    last = spread(jnp.concatenate([m2, m1], axis=0), "z", Z)
    out = correct(x0, early, partner(early, "c"), slice(2, 4))
    out, last = lax.optimization_barrier((out, last))
    return correct(out, last, partner(last, "c"), slice(0, 2))


def solution(mesh):
    fine = Mesh(mesh.devices.reshape(SIZES), AXES)
    row = P(AXES, None)
    level = P(None, AXES, None)
    return jax.shard_map(
        local,
        mesh=fine,
        in_specs=(row, row, level, level, row, row, row, row),
        out_specs=row,
        check_vma=False,
    )
```

```python
import jax
import jax.numpy as jnp
from jax import lax
from jax.experimental import pallas as pl
from jax.experimental.pallas import tpu as pltpu
from jax.sharding import Mesh, PartitionSpec as P

AXES = ("xh", "xl", "yh", "yl", "z", "c")
SIZES = (2, 2, 2, 2, 8, 2)
Z = 8
STEPS = 4
F32 = jnp.float32
BF16 = jnp.bfloat16
PAIRS = ((3, 4), (2, 4), (1, 4), (2, 3), (1, 3), (1, 2))
DIRECT = (4, (3, 4), (2, 4), (1, 4))
SHARED = (3, (2, 3), (1, 3), 2, 1, (1, 2))


def dot(a, b, dims):
    return lax.dot_general(a, b, ((dims[0], dims[1]), ((), ())), preferred_element_type=F32)


def fdot(a, b, dims):
    return lax.dot_general(
        a, b, ((dims[0], dims[1]), ((), ())), precision=lax.Precision.HIGH, preferred_element_type=F32
    )


def pack_kernel(a_ref, b_ref, c_ref, d_ref, out_ref):
    for z in range(Z):
        out_ref[z, 0:16, :] = a_ref[...]
        out_ref[z, 16:24, :] = b_ref[...]
        out_ref[z, 24:28, :] = c_ref[...]
        out_ref[z, 28:30, :] = d_ref[...]
        out_ref[z, 30:32, :] = jnp.zeros((2, 512), F32)


def pack(k4, k3, k2, k1):
    return pl.pallas_call(pack_kernel, out_shape=jax.ShapeDtypeStruct((Z, 32, 512), F32), name="pack")(k4, k3, k2, k1)


def leaf_kernel(
    core_ref, pair_ref, inv_hbm, rhs_hbm, v_hbm, w_hbm, x_hbm, keep_hbm, give_hbm, keep_shared_hbm, give_shared_hbm,
    x_ref, keep_ref, give_ref, keep_shared_ref, give_shared_ref, inv_ref, rhs_ref, v_ref, w_ref, high_ref, low_ref, sems,
):
    rows = 1024 // STEPS
    count = [0]

    def load(src, dst):
        copy = pltpu.make_async_copy(src, dst, sems.at[count[0]])
        count[0] += 1
        copy.start()
        return copy

    wait_w, wait_v = {}, {}
    wait_w[4] = load(w_hbm.at[3], w_ref.at[2])
    wait_v[3] = load(v_hbm.at[2], v_ref.at[2])
    wait_v[2] = load(v_hbm.at[1], v_ref.at[1])
    wait_v[1] = load(v_hbm.at[0], v_ref.at[0])
    wait_w[3] = load(w_hbm.at[2], w_ref.at[1])
    wait_w[2] = load(w_hbm.at[1], w_ref.at[0])
    wait_rhs = load(rhs_hbm, rhs_ref)
    parts = [pl.ds(step * rows, rows) for step in range(STEPS)]
    wait_inv = [load(inv_hbm.at[part], inv_ref.at[part]) for part in parts]
    wait_v[4] = load(v_hbm.at[3], v_ref.at[3])
    first_core = core_ref[0] == 0
    first_lanes = pair_ref[0] == 0

    def store(name, value):
        low, high = value[:128], value[128:]
        keep = jnp.where(first_core, low, high).reshape(Z, 16, 256)
        give = jnp.where(first_core, high, low).reshape(Z, 16, 256)
        if name in DIRECT:
            n = DIRECT.index(name)
            keep_ref[:, n] = keep
            give_ref[:, n] = give
            stores.append(load(give_ref.at[:, n], give_hbm.at[:, n]))
            stores.append(load(keep_ref.at[:, n], keep_hbm.at[:, n]))
            return
        n = SHARED.index(name)
        for value, ref in ((keep, keep_shared_ref), (give, give_shared_ref)):
            left, right = value[:, :, :128], value[:, :, 128:]
            ref[0, :, n] = jnp.where(first_lanes, left, right)
            ref[1, :, n] = jnp.where(first_lanes, right, left)
        stores.append(load(give_shared_ref.at[:, :, n], give_shared_hbm.at[:, :, n]))
        stores.append(load(keep_shared_ref.at[:, :, n], keep_shared_hbm.at[:, :, n]))

    stores = []
    done = set()

    def ready(waits, level):
        if (id(waits), level) not in done:
            done.add((id(waits), level))
            waits[level].wait()

    turned = {}
    for j, k in PAIRS:
        ready(wait_w, k)
        if k not in turned:
            turned[k] = w_ref[k - 2].T
        ready(wait_v, j)
        store((j, k), dot(turned[k], v_ref[j - 1], ((1,), (0,))))
    wait_rhs.wait()
    rhs = rhs_ref[...]
    rhs_turned = rhs.T
    for step, part in enumerate(parts):
        wait_inv[step].wait()
        inv = inv_ref[part, :]
        x_ref[part, :] = jnp.dot(inv, rhs, preferred_element_type=F32)
        stores.append(load(x_ref.at[part], x_hbm.at[part]))
        xt = dot(rhs_turned, inv, ((1,), (1,)))
        high = xt.astype(BF16)
        high_ref[:, part] = high
        low_ref[:, part] = (xt - high.astype(F32)).astype(BF16)
    for j in (4, 3, 2, 1):
        ready(wait_v, j)
        v = v_ref[j - 1]
        store(j, dot(high_ref[...], v, ((1,), (0,))) + dot(low_ref[...], v, ((1,), (0,))))
    for copy in stores:
        copy.wait()


def leaf(core, pair, leaf_inv, right_side, right_basis, left_basis):
    any_space = pl.BlockSpec(memory_space=pl.ANY)
    direct, shared = (Z, 4, 16, 256), (2, Z, 6, 16, 128)
    shapes = [(1024, 256), direct, direct, shared, shared]
    return pl.pallas_call(
        leaf_kernel,
        in_specs=[pl.BlockSpec(memory_space=pltpu.SMEM)] * 2 + [any_space] * 4,
        out_specs=[any_space] * 5,
        out_shape=[jax.ShapeDtypeStruct(shape, F32) for shape in shapes],
        scratch_shapes=[pltpu.VMEM(shape, F32) for shape in shapes]
        + [
            pltpu.VMEM((1024, 1024), BF16),
            pltpu.VMEM((1024, 256), BF16),
            pltpu.VMEM((4, 1024, 256), BF16),
            pltpu.VMEM((3, 1024, 256), BF16),
            pltpu.VMEM((256, 1024), BF16),
            pltpu.VMEM((256, 1024), BF16),
            pltpu.SemaphoreType.DMA((28 + 2 * STEPS,)),
        ],
        name="leaf",
    )(core.reshape(1), pair.reshape(1), leaf_inv, right_side, right_basis, left_basis)


def offsets(bit, step):
    return jnp.where(bit == 0, 0, step), jnp.where(bit == 0, step, 0)


def pair(core_ref, own, other):
    first = core_ref[0] == 0
    return jnp.where(first, own, other), jnp.where(first, other, own)


def fine_kernel(core_ref, yl_ref, rows, rows_c, a, a_c, k4_ref, k3_ref):
    near, far = offsets(yl_ref[0], 1)
    for z in range(Z):
        low, high = pair(core_ref, rows[z, 0:16], rows_c[z, 0:16])
        k4_ref[32 * z : 32 * z + 16] = low
        k4_ref[32 * z + 16 : 32 * z + 32] = high
        for t, own, other in ((near, rows[z, 16:24], rows_c[z, 16:24]), (far, a[z, 0:8], a_c[z, 0:8])):
            both = jnp.concatenate(pair(core_ref, own, other), axis=0)
            k3_ref[pl.ds(pl.multiple_of(128 * t + 16 * z, 16), 16)] = both


def coarse_kernel(core_ref, yl_ref, yh_ref, xl_ref, rows, rows_c, a, a_c, b, b_c, e, e_c, k2_ref, k1_ref):
    near, far = offsets(yl_ref[0], 1)
    up, down = offsets(yh_ref[0], 2)
    left, right = offsets(xl_ref[0], 4)

    def both(own, other):
        return jnp.concatenate(pair(core_ref, own, other), axis=0)

    for z in range(Z):
        for t, own, other in (
            (up + near, rows[z, 24:28], rows_c[z, 24:28]),
            (up + far, a[z, 8:12], a_c[z, 8:12]),
            (down + near, b[z, 0:4], b_c[z, 0:4]),
            (down + far, b[z, 8:12], b_c[z, 8:12]),
        ):
            k2_ref[pl.ds(pl.multiple_of(64 * t + 8 * z, 8), 8)] = both(own, other)
    for z in range(0, Z, 2):
        for t, (own, other, row) in (
            (left + up + near, (rows, rows_c, 28)),
            (left + up + far, (a, a_c, 12)),
            (left + down + near, (b, b_c, 4)),
            (left + down + far, (b, b_c, 12)),
            (right + up + near, (e, e_c, 0)),
            (right + up + far, (e, e_c, 2)),
            (right + down + near, (e, e_c, 4)),
            (right + down + far, (e, e_c, 6)),
        ):
            tile = [both(own[y, row : row + 2], other[y, row : row + 2]) for y in (z, z + 1)]
            k1_ref[pl.ds(pl.multiple_of(32 * t + 4 * z, 8), 8)] = jnp.concatenate(tile, axis=0)


def assemble(kernel, scalars, pieces):
    return pl.pallas_call(
        kernel,
        in_specs=[pl.BlockSpec(memory_space=pltpu.SMEM)] * len(scalars) + [pl.BlockSpec()] * len(pieces),
        out_shape=[jax.ShapeDtypeStruct((256, 512), F32)] * 2,
    )(*[scalar.reshape(1) for scalar in scalars], *pieces)


def partner(block, axis):
    return lax.ppermute(block, axis, [(0, 1), (1, 0)])


def ordered(bit, own, other, axis):
    low = jnp.where(bit == 0, own, other)
    high = jnp.where(bit == 0, other, own)
    return jnp.concatenate([low, high], axis=axis)


def exchange(block, axes):
    return lax.all_to_all(block, axes, 0, 0, tiled=True)


def spread(block, axes, count):
    return exchange(jnp.broadcast_to(block[None], (count,) + block.shape), axes)


def local(right_side, leaf_inv, right_basis, left_basis, k1, k2, k3, k4):
    at = {axis: lax.axis_index(axis) for axis in AXES}
    core = at["c"]
    rows = exchange(pack(k4, k3, k2, k1), "z")
    x0, keep, give, keep_shared, give_shared = leaf(
        core, at["yl"], leaf_inv, right_side, right_basis, left_basis
    )
    mine = partner(give, "c")
    mine = keep + mine
    got_shared = partner(give_shared, "c")
    got = partner(keep_shared[1] + got_shared[1], "yl")
    direct = exchange(mine, "z")
    pairs = (keep_shared[0] + got_shared[0]) + got
    pairs, rows = lax.optimization_barrier((pairs, rows))
    upper = at["yh"] == 0
    fours = pairs[:, 3:5]
    give = jnp.where(upper, fours[:, :, 8:], fours[:, :, :8]).reshape(Z, 1, 16, 128)
    got = partner(jnp.concatenate([give, pairs[:, 5:]], axis=1), "yh")
    keep = jnp.where(upper, fours[:, :, :8], fours[:, :, 8:]).reshape(Z, 1, 16, 128)
    fours = jnp.concatenate([keep, pairs[:, 5:]], axis=1) + got
    rows_c = partner(rows, "c")
    a0 = rows[:, 16:32]
    a1 = partner(a0, "yl")
    a1_c = partner(a1, "c")
    b0 = jnp.concatenate([a0[:, 8:], a1[:, 8:]], axis=1)
    b1 = partner(b0, "yh")
    b1_c = partner(b1, "c")
    e0 = jnp.concatenate([b0[:, 4:6], b0[:, 12:14], b1[:, 4:6], b1[:, 12:14]], axis=1)
    e1 = partner(e0, "xl")
    e1_c = partner(e1, "c")
    pieces = [rows, rows_c, a1, a1_c]
    full4, full3 = assemble(fine_kernel, [core, at["yl"]], pieces)
    scalars = [at[axis] for axis in ("c", "yl", "yh", "xl")]
    full2, full1 = assemble(coarse_kernel, scalars, pieces + [b1, b1_c, e1, e1_c])

    def both_cores(own, other, first, count):
        own = own[:, first : first + count].reshape(Z * count, -1)
        other = other[:, first : first + count].reshape(Z * count, -1)
        return ordered(core, own, other, 0)

    def mix(k, own, other, axis):
        return fdot(ordered(at[axis], own, other, 1), k, ((1,), (1,)))

    def of_four(block, axes):
        far, near, last = [lax.ppermute(block, axes, [(i, i ^ k) for i in range(4)]) for k in (2, 1, 3)]
        return [block, near, far, last]

    def times(m, g):
        return fdot(m, g, ((1,), (0,)))

    def in_lanes(block):
        zero = jnp.zeros_like(block)
        first = at["yl"] == 0
        return jnp.concatenate([jnp.where(first, block, zero), jnp.where(first, zero, block)], axis=1)

    def in_rows(block):
        zero = jnp.zeros_like(block)
        return jnp.concatenate([jnp.where(upper, block, zero), jnp.where(upper, zero, block)], axis=0)

    direct = direct.sum(axis=0)
    to_all = jnp.broadcast_to(jnp.concatenate([direct[1:, :, :128], direct[1:, :, 128:]], axis=0)[None], (Z, 6, 16, 128))
    mixed = jnp.concatenate(
        [to_all.reshape(Z, 96, 128), pairs[:, :3].reshape(Z, 48, 128), fours.reshape(Z, 32, 128)], axis=1
    )
    mixed = exchange(mixed, "z")
    m4 = mix(full4, direct[0], partner(direct[0], "yl"), "yl")
    own = mixed[:, :96]
    other = partner(own, "c")
    g34, g24, g14 = [
        jnp.concatenate([both_cores(own, other, 16 * n, 16), both_cores(own, other, 48 + 16 * n, 16)], axis=1)
        for n in range(3)
    ]
    sums = mixed[:, 96:].sum(axis=0)
    third = spread(jnp.concatenate([sums[16:48], sums[64:80]], axis=0), "z", Z)
    t = in_lanes(sums[0:16]) - times(m4, g34)
    got = partner(t, "yl")
    t = t + got
    m3 = mix(full3, t, partner(t, "yh"), "yh")
    own, m3 = lax.optimization_barrier((third, m3))
    t2 = in_rows(in_lanes(sums[48:56])) - times(m4, g24)
    t1 = in_rows(in_lanes(sums[56:64])) - times(m4, g14)
    other = partner(own, "c")
    g23, g13 = both_cores(own, other, 0, 16), both_cores(own, other, 16, 16)
    half = both_cores(own, other, 32, 16)
    g12 = ordered(at["yl"], half, partner(half, "yl"), 1)
    t = jnp.stack([t2 - in_lanes(times(m3, g23)), t1 - in_lanes(times(m3, g13))])
    four = of_four(t, ("yh", "yl"))
    t = (four[0] + four[1]) + (four[2] + four[3])
    m2 = mix(full2, t[0], partner(t[0], "xl"), "xl")
    four = of_four(t[1] - times(m2, g12), ("xh", "xl"))
    m1 = mix(full1, four[0] + four[1], four[2] + four[3], "xh")

    own = spread(jnp.concatenate([m4, m3, m2, m1], axis=0), "z", Z)
    other = partner(own, "c")
    m = jnp.stack([both_cores(own, other, 16 * n, 16) for n in (3, 2, 1, 0)])
    high = lax.reduce_precision(m, 8, 7)
    low = (m - high).astype(BF16)
    dims = ((0, 2), (0, 2))
    return x0 - (dot(left_basis, high.astype(BF16), dims) + dot(left_basis, low, dims))


def solution(mesh):
    fine = Mesh(mesh.devices.reshape(SIZES), AXES)
    row = P(AXES, None)
    level = P(None, AXES, None)
    return jax.shard_map(
        local,
        mesh=fine,
        in_specs=(row, row, level, level, row, row, row, row),
        out_specs=row,
        check_vma=False,
    )
```

```python
import jax
import jax.numpy as jnp
from jax import lax
from jax.experimental import pallas as pl
from jax.experimental.pallas import tpu as pltpu
from jax.sharding import Mesh, PartitionSpec as P

AXES = ("xh", "xl", "yh", "yl", "z", "c")
SIZES = (2, 2, 2, 2, 8, 2)
Z = 8
STEPS = 4
F32 = jnp.float32
BF16 = jnp.bfloat16
DIRECT = (4, (3, 4), (2, 4), (1, 4))
SHARED = (3, (2, 3), (1, 3), 2, 1, (1, 2))


def dot(a, b, dims):
    return lax.dot_general(a, b, ((dims[0], dims[1]), ((), ())), preferred_element_type=F32)


def fdot(a, b, dims):
    return lax.dot_general(
        a, b, ((dims[0], dims[1]), ((), ())), precision=lax.Precision.HIGH, preferred_element_type=F32
    )


def pack_kernel(a_ref, b_ref, c_ref, d_ref, out_ref):
    for z in range(Z):
        out_ref[z, 0:16, :] = a_ref[...]
        out_ref[z, 16:24, :] = b_ref[...]
        out_ref[z, 24:28, :] = c_ref[...]
        out_ref[z, 28:30, :] = d_ref[...]
        out_ref[z, 30:32, :] = jnp.zeros((2, 512), F32)


def pack(k4, k3, k2, k1):
    return pl.pallas_call(pack_kernel, out_shape=jax.ShapeDtypeStruct((Z, 32, 512), F32), name="pack")(k4, k3, k2, k1)


def leaf_kernel(
    core_ref, pair_ref, inv_hbm, rhs_hbm, v_hbm, w_hbm, x_hbm, keep_hbm, give_hbm, keep_shared_hbm, give_shared_hbm,
    x_ref, keep_ref, give_ref, keep_shared_ref, give_shared_ref, inv_ref, rhs_ref, v_ref, w_ref, left_ref, split_ref, sems,
):
    rows = 1024 // STEPS
    count = [0]

    def load(src, dst):
        copy = pltpu.make_async_copy(src, dst, sems.at[count[0]])
        count[0] += 1
        copy.start()
        return copy

    wait_w, wait_v = {}, {}
    wait_w[4] = load(w_hbm.at[3], w_ref.at[2])
    wait_v[3] = load(v_hbm.at[2], v_ref.at[2])
    wait_v[2] = load(v_hbm.at[1], v_ref.at[1])
    wait_v[1] = load(v_hbm.at[0], v_ref.at[0])
    wait_w[3] = load(w_hbm.at[2], w_ref.at[1])
    wait_w[2] = load(w_hbm.at[1], w_ref.at[0])
    wait_rhs = load(rhs_hbm, rhs_ref)
    parts = [pl.ds(step * rows, rows) for step in range(STEPS)]
    wait_inv = [load(inv_hbm.at[part], inv_ref.at[part]) for part in parts]
    wait_v[4] = load(v_hbm.at[3], v_ref.at[3])
    first_core = core_ref[0] == 0
    first_lanes = pair_ref[0] == 0

    def store(name, value):
        low, high = value[:128], value[128:]
        keep = jnp.where(first_core, low, high).reshape(Z, 16, 256)
        give = jnp.where(first_core, high, low).reshape(Z, 16, 256)
        if name in DIRECT:
            n = DIRECT.index(name)
            keep_ref[:, n] = keep
            give_ref[:, n] = give
            stores.append(load(give_ref.at[:, n], give_hbm.at[:, n]))
            stores.append(load(keep_ref.at[:, n], keep_hbm.at[:, n]))
            return
        n = SHARED.index(name)
        for value, ref in ((keep, keep_shared_ref), (give, give_shared_ref)):
            left, right = value[:, :, :128], value[:, :, 128:]
            ref[0, :, n] = jnp.where(first_lanes, left, right)
            ref[1, :, n] = jnp.where(first_lanes, right, left)
        stores.append(load(give_shared_ref.at[:, :, n], give_shared_hbm.at[:, :, n]))
        stores.append(load(keep_shared_ref.at[:, :, n], keep_shared_hbm.at[:, :, n]))

    stores = []
    done = set()

    def ready(waits, level):
        if (id(waits), level) not in done:
            done.add((id(waits), level))
            waits[level].wait()

    for j in (3, 2, 1):
        for k in range(4, j, -1):
            if ("turned", k) not in done:
                done.add(("turned", k))
                ready(wait_w, k)
                left_ref[pl.ds(256 * (k - 2), 256), :] = w_ref[k - 2].T
        ready(wait_v, j)
        value = dot(left_ref[pl.ds(256 * (j - 1), 256 * (4 - j)), :], v_ref[j - 1], ((1,), (0,)))
        for k in range(j + 1, 5):
            store((j, k), value[256 * (k - j - 1) : 256 * (k - j)])
    wait_rhs.wait()
    rhs = rhs_ref[...]
    rhs_turned = rhs.T
    for step, part in enumerate(parts):
        wait_inv[step].wait()
        inv = inv_ref[part, :]
        x_ref[part, :] = jnp.dot(inv, rhs, preferred_element_type=F32)
        stores.append(load(x_ref.at[part], x_hbm.at[part]))
        xt = dot(rhs_turned, inv, ((1,), (1,)))
        high = xt.astype(BF16)
        split_ref[0:256, part] = high
        split_ref[256:512, part] = (xt - high.astype(F32)).astype(BF16)
    for j in (4, 3, 2, 1):
        ready(wait_v, j)
        v = v_ref[j - 1]
        both = dot(split_ref[...], v, ((1,), (0,)))
        store(j, both[:256] + both[256:])
    for copy in stores:
        copy.wait()


def leaf(core, pair, leaf_inv, right_side, right_basis, left_basis):
    any_space = pl.BlockSpec(memory_space=pl.ANY)
    direct, shared = (Z, 4, 16, 256), (2, Z, 6, 16, 128)
    shapes = [(1024, 256), direct, direct, shared, shared]
    return pl.pallas_call(
        leaf_kernel,
        in_specs=[pl.BlockSpec(memory_space=pltpu.SMEM)] * 2 + [any_space] * 4,
        out_specs=[any_space] * 5,
        out_shape=[jax.ShapeDtypeStruct(shape, F32) for shape in shapes],
        scratch_shapes=[pltpu.VMEM(shape, F32) for shape in shapes]
        + [
            pltpu.VMEM((1024, 1024), BF16),
            pltpu.VMEM((1024, 256), BF16),
            pltpu.VMEM((4, 1024, 256), BF16),
            pltpu.VMEM((3, 1024, 256), BF16),
            pltpu.VMEM((768, 1024), BF16),
            pltpu.VMEM((512, 1024), BF16),
            pltpu.SemaphoreType.DMA((28 + 2 * STEPS,)),
        ],
        name="leaf",
    )(core.reshape(1), pair.reshape(1), leaf_inv, right_side, right_basis, left_basis)


def offsets(bit, step):
    return jnp.where(bit == 0, 0, step), jnp.where(bit == 0, step, 0)


def pair(core_ref, own, other):
    first = core_ref[0] == 0
    return jnp.where(first, own, other), jnp.where(first, other, own)


def fine_kernel(core_ref, yl_ref, rows, rows_c, a, a_c, k4_ref, k3_ref):
    near, far = offsets(yl_ref[0], 1)
    for z in range(Z):
        low, high = pair(core_ref, rows[z, 0:16], rows_c[z, 0:16])
        k4_ref[32 * z : 32 * z + 16] = low
        k4_ref[32 * z + 16 : 32 * z + 32] = high
        for t, own, other in ((near, rows[z, 16:24], rows_c[z, 16:24]), (far, a[z], a_c[z])):
            both = jnp.concatenate(pair(core_ref, own, other), axis=0)
            k3_ref[pl.ds(pl.multiple_of(128 * t + 16 * z, 16), 16)] = both


def coarse_kernel(core_ref, yl_ref, yh_ref, xl_ref, rows, rows_c, a, a_c, b, b_c, e, e_c, k2_ref, k1_ref):
    near, far = offsets(yl_ref[0], 1)
    up, down = offsets(yh_ref[0], 2)
    left, right = offsets(xl_ref[0], 4)

    def both(own, other):
        return jnp.concatenate(pair(core_ref, own, other), axis=0)

    for z in range(Z):
        for t, own, other in (
            (up + near, rows[z, 0:4], rows_c[z, 0:4]),
            (up + far, a[z, 0:4], a_c[z, 0:4]),
            (down + near, b[z, 0:4], b_c[z, 0:4]),
            (down + far, b[z, 8:12], b_c[z, 8:12]),
        ):
            k2_ref[pl.ds(pl.multiple_of(64 * t + 8 * z, 8), 8)] = both(own, other)
    for z in range(0, Z, 2):
        for t, (own, other, row) in (
            (left + up + near, (rows, rows_c, 4)),
            (left + up + far, (a, a_c, 4)),
            (left + down + near, (b, b_c, 4)),
            (left + down + far, (b, b_c, 12)),
            (right + up + near, (e, e_c, 0)),
            (right + up + far, (e, e_c, 2)),
            (right + down + near, (e, e_c, 4)),
            (right + down + far, (e, e_c, 6)),
        ):
            tile = [both(own[y, row : row + 2], other[y, row : row + 2]) for y in (z, z + 1)]
            k1_ref[pl.ds(pl.multiple_of(32 * t + 4 * z, 8), 8)] = jnp.concatenate(tile, axis=0)


def assemble(kernel, scalars, pieces, blocks):
    specs = [pl.BlockSpec((Z, count, 512), lambda i, index=index: (0, index, 0)) for count, index in blocks]
    full = pl.BlockSpec((256, 512), lambda i: (0, 0))
    return pl.pallas_call(
        kernel,
        grid=(1,),
        in_specs=[pl.BlockSpec(memory_space=pltpu.SMEM)] * len(scalars) + specs,
        out_specs=[full, full],
        out_shape=[jax.ShapeDtypeStruct((256, 512), F32)] * 2,
    )(*[scalar.reshape(1) for scalar in scalars], *pieces)


def partner(block, axis):
    return lax.ppermute(block, axis, [(0, 1), (1, 0)])


def ordered(bit, own, other, axis):
    low = jnp.where(bit == 0, own, other)
    high = jnp.where(bit == 0, other, own)
    return jnp.concatenate([low, high], axis=axis)


def exchange(block, axes):
    return lax.all_to_all(block, axes, 0, 0, tiled=True)


def spread(block, axes, count):
    return exchange(jnp.broadcast_to(block[None], (count,) + block.shape), axes)


def local(right_side, leaf_inv, right_basis, left_basis, k1, k2, k3, k4):
    at = {axis: lax.axis_index(axis) for axis in AXES}
    core = at["c"]
    rows = exchange(pack(k4, k3, k2, k1), "z")
    x0, keep, give, keep_shared, give_shared = leaf(
        core, at["yl"], leaf_inv, right_side, right_basis, left_basis
    )
    mine = partner(give, "c")
    mine = keep + mine
    got_shared = partner(give_shared, "c")
    got = partner(keep_shared[1] + got_shared[1], "yl")
    direct = exchange(mine, "z")
    pairs = (keep_shared[0] + got_shared[0]) + got
    pairs, rows = lax.optimization_barrier((pairs, rows))
    upper = at["yh"] == 0
    fours = pairs[:, 3:5]
    give = jnp.where(upper, fours[:, :, 8:], fours[:, :, :8]).reshape(Z, 1, 16, 128)
    got = partner(jnp.concatenate([give, pairs[:, 5:]], axis=1), "yh")
    keep = jnp.where(upper, fours[:, :, :8], fours[:, :, 8:]).reshape(Z, 1, 16, 128)
    fours = jnp.concatenate([keep, pairs[:, 5:]], axis=1) + got
    rows_c = partner(rows, "c")
    a0 = rows[:, 16:32]
    a1 = partner(a0, "yl")
    a1_c = partner(a1, "c")
    b0 = jnp.concatenate([a0[:, 8:], a1[:, 8:]], axis=1)
    b1 = partner(b0, "yh")
    b1_c = partner(b1, "c")
    e0 = jnp.concatenate([b0[:, 4:6], b0[:, 12:14], b1[:, 4:6], b1[:, 12:14]], axis=1)
    e1 = partner(e0, "xl")
    e1_c = partner(e1, "c")
    pieces = [rows, rows_c, a1, a1_c]
    full4, full3 = assemble(fine_kernel, [core, at["yl"]], pieces, [(32, 0)] * 2 + [(8, 0)] * 2)
    scalars = [at[axis] for axis in ("c", "yl", "yh", "xl")]
    full2, full1 = assemble(
        coarse_kernel, scalars, pieces + [b1, b1_c, e1, e1_c], [(8, 3)] * 2 + [(8, 1)] * 2 + [(16, 0)] * 2 + [(8, 0)] * 2
    )

    def both_cores(own, other, first, count):
        own = own[:, first : first + count].reshape(Z * count, -1)
        other = other[:, first : first + count].reshape(Z * count, -1)
        return ordered(core, own, other, 0)

    def mix(k, own, other, axis):
        return fdot(ordered(at[axis], own, other, 1), k, ((1,), (1,)))

    def of_four(block, axes):
        got = {}
        for k in (2, 1, 3):
            got[k] = lax.ppermute(block, axes, [(i, i ^ k) for i in range(4)])
        return [block, got[1], got[2], got[3]]

    def times(m, g):
        return fdot(m, g, ((1,), (0,)))

    def in_lanes(block):
        zero = jnp.zeros_like(block)
        first = at["yl"] == 0
        return jnp.concatenate([jnp.where(first, block, zero), jnp.where(first, zero, block)], axis=1)

    def in_rows(block):
        zero = jnp.zeros_like(block)
        return jnp.concatenate([jnp.where(upper, block, zero), jnp.where(upper, zero, block)], axis=0)

    direct = direct.sum(axis=0)
    to_all = jnp.broadcast_to(jnp.concatenate([direct[1:, :, :128], direct[1:, :, 128:]], axis=0)[None], (Z, 6, 16, 128))
    mixed = jnp.concatenate(
        [to_all.reshape(Z, 96, 128), pairs[:, :3].reshape(Z, 48, 128), fours.reshape(Z, 32, 128)], axis=1
    )
    mixed = exchange(mixed, "z")
    m4 = mix(full4, direct[0], partner(direct[0], "yl"), "yl")
    own = mixed[:, :96]
    other = partner(own, "c")
    g34, g24, g14 = [
        jnp.concatenate([both_cores(own, other, 16 * n, 16), both_cores(own, other, 48 + 16 * n, 16)], axis=1)
        for n in range(3)
    ]
    sums = mixed[:, 96:].sum(axis=0)
    third = spread(jnp.concatenate([sums[16:48], sums[64:80]], axis=0), "z", Z)
    t = in_lanes(sums[0:16]) - times(m4, g34)
    got = partner(t, "yl")
    t = t + got
    m3 = mix(full3, t, partner(t, "yh"), "yh")
    own, m3 = lax.optimization_barrier((third, m3))
    t2 = in_rows(in_lanes(sums[48:56])) - times(m4, g24)
    t1 = in_rows(in_lanes(sums[56:64])) - times(m4, g14)
    other = partner(own, "c")
    g23, g13 = both_cores(own, other, 0, 16), both_cores(own, other, 16, 16)
    half = both_cores(own, other, 32, 16)
    got = partner(half, "yl")
    g12 = ordered(at["yl"], half, got, 1)
    t = jnp.stack([t2 - in_lanes(times(m3, g23)), t1 - in_lanes(times(m3, g13))])
    four = of_four(t, ("yh", "yl"))
    t = (four[0] + four[1]) + (four[2] + four[3])
    m2 = mix(full2, t[0], partner(t[0], "xl"), "xl")
    four = of_four(t[1] - times(m2, g12), ("xh", "xl"))
    m1 = mix(full1, four[0] + four[1], four[2] + four[3], "xh")

    own = spread(jnp.concatenate([m4, m3, m2, m1], axis=0), "z", Z)
    other = partner(own, "c")
    m = jnp.stack([both_cores(own, other, 16 * n, 16) for n in (3, 2, 1, 0)])
    high = lax.reduce_precision(m, 8, 7)
    low = (m - high).astype(BF16)
    dims = ((0, 2), (0, 2))
    return x0 - (dot(left_basis, high.astype(BF16), dims) + dot(left_basis, low, dims))


def solution(mesh):
    fine = Mesh(mesh.devices.reshape(SIZES), AXES)
    row = P(AXES, None)
    level = P(None, AXES, None)
    return jax.shard_map(
        local,
        mesh=fine,
        in_specs=(row, row, level, level, row, row, row, row),
        out_specs=row,
        check_vma=False,
    )
```

```python
import jax
import jax.numpy as jnp
from jax import lax
from jax.experimental import pallas as pl
from jax.experimental.pallas import tpu as pltpu
from jax.sharding import Mesh, PartitionSpec as P

AXES = ("xh", "xl", "yh", "yl", "z", "c")
SIZES = (2, 2, 2, 2, 8, 2)
Z = 8
STEPS = 4
F32 = jnp.float32
BF16 = jnp.bfloat16
PAIRS = ((3, 4), (2, 4), (1, 4), (2, 3), (1, 3), (1, 2))
DIRECT = (4, (3, 4), (2, 4), (1, 4))
SHARED = (3, (2, 3), (1, 3), 2, 1, (1, 2))


def dot(a, b, dims):
    return lax.dot_general(a, b, ((dims[0], dims[1]), ((), ())), preferred_element_type=F32)


def fdot(a, b, dims):
    return lax.dot_general(
        a, b, ((dims[0], dims[1]), ((), ())), precision=lax.Precision.HIGH, preferred_element_type=F32
    )


def pack_kernel(a_ref, b_ref, c_ref, d_ref, out_ref):
    for z in range(Z):
        out_ref[z, 0:16, :] = a_ref[...]
        out_ref[z, 16:24, :] = b_ref[...]
        out_ref[z, 24:28, :] = c_ref[...]
        out_ref[z, 28:30, :] = d_ref[...]
        out_ref[z, 30:32, :] = jnp.zeros((2, 512), F32)


def pack(k4, k3, k2, k1):
    return pl.pallas_call(pack_kernel, out_shape=jax.ShapeDtypeStruct((Z, 32, 512), F32), name="pack")(k4, k3, k2, k1)


def leaf_kernel(
    core_ref, pair_ref, inv_hbm, rhs_hbm, v_hbm, w_hbm, x_hbm, keep_hbm, give_hbm, keep_shared_hbm, give_shared_hbm,
    x_ref, keep_ref, give_ref, keep_shared_ref, give_shared_ref, inv_ref, rhs_ref, v_ref, w_ref, high_ref, low_ref, sems,
):
    rows = 1024 // STEPS
    count = [0]

    def load(src, dst):
        copy = pltpu.make_async_copy(src, dst, sems.at[count[0]])
        count[0] += 1
        copy.start()
        return copy

    wait_w, wait_v = {}, {}
    wait_w[4] = load(w_hbm.at[3], w_ref.at[2])
    wait_v[3] = load(v_hbm.at[2], v_ref.at[2])
    wait_v[2] = load(v_hbm.at[1], v_ref.at[1])
    wait_v[1] = load(v_hbm.at[0], v_ref.at[0])
    wait_w[3] = load(w_hbm.at[2], w_ref.at[1])
    wait_w[2] = load(w_hbm.at[1], w_ref.at[0])
    wait_rhs = load(rhs_hbm, rhs_ref)
    parts = [pl.ds(step * rows, rows) for step in range(STEPS)]
    wait_inv = [load(inv_hbm.at[part], inv_ref.at[part]) for part in parts]
    wait_v[4] = load(v_hbm.at[3], v_ref.at[3])
    first_core = core_ref[0] == 0
    first_lanes = pair_ref[0] == 0

    def store(name, value):
        low, high = value[:128], value[128:]
        keep = jnp.where(first_core, low, high).reshape(Z, 16, 256)
        give = jnp.where(first_core, high, low).reshape(Z, 16, 256)
        if name in DIRECT:
            n = DIRECT.index(name)
            keep_ref[:, n] = keep
            give_ref[:, n] = give
            stores.append(load(give_ref.at[:, n], give_hbm.at[:, n]))
            stores.append(load(keep_ref.at[:, n], keep_hbm.at[:, n]))
            return
        n = SHARED.index(name)
        for value, ref in ((keep, keep_shared_ref), (give, give_shared_ref)):
            left, right = value[:, :, :128], value[:, :, 128:]
            ref[0, :, n] = jnp.where(first_lanes, left, right)
            ref[1, :, n] = jnp.where(first_lanes, right, left)
        stores.append(load(give_shared_ref.at[:, :, n], give_shared_hbm.at[:, :, n]))
        stores.append(load(keep_shared_ref.at[:, :, n], keep_shared_hbm.at[:, :, n]))

    stores = []
    done = set()

    def ready(waits, level):
        if (id(waits), level) not in done:
            done.add((id(waits), level))
            waits[level].wait()

    turned = {}
    for j, k in PAIRS:
        ready(wait_w, k)
        if k not in turned:
            turned[k] = w_ref[k - 2].T
        ready(wait_v, j)
        store((j, k), dot(turned[k], v_ref[j - 1], ((1,), (0,))))
    wait_rhs.wait()
    rhs = rhs_ref[...]
    rhs_turned = rhs.T
    for step, part in enumerate(parts):
        wait_inv[step].wait()
        inv = inv_ref[part, :]
        x_ref[part, :] = jnp.dot(inv, rhs, preferred_element_type=F32)
        stores.append(load(x_ref.at[part], x_hbm.at[part]))
        xt = dot(rhs_turned, inv, ((1,), (1,)))
        high = xt.astype(BF16)
        high_ref[:, part] = high
        low_ref[:, part] = (xt - high.astype(F32)).astype(BF16)
    for j in (4, 3, 2, 1):
        ready(wait_v, j)
        v = v_ref[j - 1]
        store(j, dot(high_ref[...], v, ((1,), (0,))) + dot(low_ref[...], v, ((1,), (0,))))
    for copy in stores:
        copy.wait()


def leaf(core, pair, leaf_inv, right_side, right_basis, left_basis):
    any_space = pl.BlockSpec(memory_space=pl.ANY)
    direct, shared = (Z, 4, 16, 256), (2, Z, 6, 16, 128)
    shapes = [(1024, 256), direct, direct, shared, shared]
    return pl.pallas_call(
        leaf_kernel,
        in_specs=[pl.BlockSpec(memory_space=pltpu.SMEM)] * 2 + [any_space] * 4,
        out_specs=[any_space] * 5,
        out_shape=[jax.ShapeDtypeStruct(shape, F32) for shape in shapes],
        scratch_shapes=[pltpu.VMEM(shape, F32) for shape in shapes]
        + [
            pltpu.VMEM((1024, 1024), BF16),
            pltpu.VMEM((1024, 256), BF16),
            pltpu.VMEM((4, 1024, 256), BF16),
            pltpu.VMEM((3, 1024, 256), BF16),
            pltpu.VMEM((256, 1024), BF16),
            pltpu.VMEM((256, 1024), BF16),
            pltpu.SemaphoreType.DMA((28 + 2 * STEPS,)),
        ],
        name="leaf",
    )(core.reshape(1), pair.reshape(1), leaf_inv, right_side, right_basis, left_basis)


def offsets(bit, step):
    return jnp.where(bit == 0, 0, step), jnp.where(bit == 0, step, 0)


def pair(core_ref, own, other):
    first = core_ref[0] == 0
    return jnp.where(first, own, other), jnp.where(first, other, own)


def fine_kernel(core_ref, yl_ref, rows, rows_c, a, a_c, k4_ref, k3_ref):
    near, far = offsets(yl_ref[0], 1)
    for z in range(Z):
        low, high = pair(core_ref, rows[z, 0:16], rows_c[z, 0:16])
        k4_ref[32 * z : 32 * z + 16] = low
        k4_ref[32 * z + 16 : 32 * z + 32] = high
        for t, own, other in ((near, rows[z, 16:24], rows_c[z, 16:24]), (far, a[z], a_c[z])):
            both = jnp.concatenate(pair(core_ref, own, other), axis=0)
            k3_ref[pl.ds(pl.multiple_of(128 * t + 16 * z, 16), 16)] = both


def coarse_kernel(core_ref, yl_ref, yh_ref, xl_ref, rows, rows_c, a, a_c, b, b_c, e, e_c, k2_ref, k1_ref):
    near, far = offsets(yl_ref[0], 1)
    up, down = offsets(yh_ref[0], 2)
    left, right = offsets(xl_ref[0], 4)

    def both(own, other):
        return jnp.concatenate(pair(core_ref, own, other), axis=0)

    for z in range(Z):
        for t, own, other in (
            (up + near, rows[z, 0:4], rows_c[z, 0:4]),
            (up + far, a[z, 0:4], a_c[z, 0:4]),
            (down + near, b[z, 0:4], b_c[z, 0:4]),
            (down + far, b[z, 8:12], b_c[z, 8:12]),
        ):
            k2_ref[pl.ds(pl.multiple_of(64 * t + 8 * z, 8), 8)] = both(own, other)
    for z in range(0, Z, 2):
        for t, (own, other, row) in (
            (left + up + near, (rows, rows_c, 4)),
            (left + up + far, (a, a_c, 4)),
            (left + down + near, (b, b_c, 4)),
            (left + down + far, (b, b_c, 12)),
            (right + up + near, (e, e_c, 0)),
            (right + up + far, (e, e_c, 2)),
            (right + down + near, (e, e_c, 4)),
            (right + down + far, (e, e_c, 6)),
        ):
            tile = [both(own[y, row : row + 2], other[y, row : row + 2]) for y in (z, z + 1)]
            k1_ref[pl.ds(pl.multiple_of(32 * t + 4 * z, 8), 8)] = jnp.concatenate(tile, axis=0)


def assemble(kernel, scalars, pieces, blocks):
    specs = [pl.BlockSpec((Z, count, 512), lambda i, index=index: (0, index, 0)) for count, index in blocks]
    full = pl.BlockSpec((256, 512), lambda i: (0, 0))
    return pl.pallas_call(
        kernel,
        grid=(1,),
        in_specs=[pl.BlockSpec(memory_space=pltpu.SMEM)] * len(scalars) + specs,
        out_specs=[full, full],
        out_shape=[jax.ShapeDtypeStruct((256, 512), F32)] * 2,
    )(*[scalar.reshape(1) for scalar in scalars], *pieces)


def partner(block, axis):
    return lax.ppermute(block, axis, [(0, 1), (1, 0)])


def ordered(bit, own, other, axis):
    low = jnp.where(bit == 0, own, other)
    high = jnp.where(bit == 0, other, own)
    return jnp.concatenate([low, high], axis=axis)


def exchange(block, axes):
    return lax.all_to_all(block, axes, 0, 0, tiled=True)


def spread(block, axes, count):
    return exchange(jnp.broadcast_to(block[None], (count,) + block.shape), axes)


def local(right_side, leaf_inv, right_basis, left_basis, k1, k2, k3, k4):
    at = {axis: lax.axis_index(axis) for axis in AXES}
    core = at["c"]
    rows = exchange(pack(k4, k3, k2, k1), "z")
    x0, keep, give, keep_shared, give_shared = leaf(
        core, at["yl"], leaf_inv, right_side, right_basis, left_basis
    )
    mine = partner(give, "c")
    mine = keep + mine
    got_shared = partner(give_shared, "c")
    got = partner(keep_shared[1] + got_shared[1], "yl")
    direct = exchange(mine, "z")
    pairs = (keep_shared[0] + got_shared[0]) + got
    pairs, rows = lax.optimization_barrier((pairs, rows))
    upper = at["yh"] == 0
    fours = pairs[:, 3:5]
    give = jnp.where(upper, fours[:, :, 8:], fours[:, :, :8]).reshape(Z, 1, 16, 128)
    got = partner(jnp.concatenate([give, pairs[:, 5:]], axis=1), "yh")
    keep = jnp.where(upper, fours[:, :, :8], fours[:, :, 8:]).reshape(Z, 1, 16, 128)
    fours = jnp.concatenate([keep, pairs[:, 5:]], axis=1) + got
    rows_c = partner(rows, "c")
    a0 = rows[:, 16:32]
    a1 = partner(a0, "yl")
    a1_c = partner(a1, "c")
    b0 = jnp.concatenate([a0[:, 8:], a1[:, 8:]], axis=1)
    b1 = partner(b0, "yh")
    b1_c = partner(b1, "c")
    e0 = jnp.concatenate([b0[:, 4:6], b0[:, 12:14], b1[:, 4:6], b1[:, 12:14]], axis=1)
    e1 = partner(e0, "xl")
    e1_c = partner(e1, "c")
    pieces = [rows, rows_c, a1, a1_c]
    full4, full3 = assemble(fine_kernel, [core, at["yl"]], pieces, [(32, 0)] * 2 + [(8, 0)] * 2)
    scalars = [at[axis] for axis in ("c", "yl", "yh", "xl")]
    full2, full1 = assemble(
        coarse_kernel, scalars, pieces + [b1, b1_c, e1, e1_c], [(8, 3)] * 2 + [(8, 1)] * 2 + [(16, 0)] * 2 + [(8, 0)] * 2
    )

    def both_cores(own, other, first, count):
        own = own[:, first : first + count].reshape(Z * count, -1)
        other = other[:, first : first + count].reshape(Z * count, -1)
        return ordered(core, own, other, 0)

    def mix(k, own, other, axis):
        return fdot(ordered(at[axis], own, other, 1), k, ((1,), (1,)))

    def of_four(block, axes):
        got = {}
        for k in (2, 1, 3):
            got[k] = lax.ppermute(block, axes, [(i, i ^ k) for i in range(4)])
        return [block, got[1], got[2], got[3]]

    def times(m, g):
        return fdot(m, g, ((1,), (0,)))

    def in_lanes(block):
        zero = jnp.zeros_like(block)
        first = at["yl"] == 0
        return jnp.concatenate([jnp.where(first, block, zero), jnp.where(first, zero, block)], axis=1)

    def in_rows(block):
        zero = jnp.zeros_like(block)
        return jnp.concatenate([jnp.where(upper, block, zero), jnp.where(upper, zero, block)], axis=0)

    direct = direct.sum(axis=0)
    to_all = jnp.broadcast_to(jnp.concatenate([direct[1:, :, :128], direct[1:, :, 128:]], axis=0)[None], (Z, 6, 16, 128))
    mixed = jnp.concatenate(
        [to_all.reshape(Z, 96, 128), pairs[:, :3].reshape(Z, 48, 128), fours.reshape(Z, 32, 128)], axis=1
    )
    mixed = exchange(mixed, "z")
    m4 = mix(full4, direct[0], partner(direct[0], "yl"), "yl")
    own = mixed[:, :96]
    other = partner(own, "c")
    g34, g24, g14 = [
        jnp.concatenate([both_cores(own, other, 16 * n, 16), both_cores(own, other, 48 + 16 * n, 16)], axis=1)
        for n in range(3)
    ]
    sums = mixed[:, 96:].sum(axis=0)
    third = spread(jnp.concatenate([sums[16:48], sums[64:80]], axis=0), "z", Z)
    t = in_lanes(sums[0:16]) - times(m4, g34)
    got = partner(t, "yl")
    t = t + got
    m3 = mix(full3, t, partner(t, "yh"), "yh")
    own, m3 = lax.optimization_barrier((third, m3))
    t2 = in_rows(in_lanes(sums[48:56])) - times(m4, g24)
    t1 = in_rows(in_lanes(sums[56:64])) - times(m4, g14)
    other = partner(own, "c")
    g23, g13 = both_cores(own, other, 0, 16), both_cores(own, other, 16, 16)
    half = both_cores(own, other, 32, 16)
    got = partner(half, "yl")
    g12 = ordered(at["yl"], half, got, 1)
    t = jnp.stack([t2 - in_lanes(times(m3, g23)), t1 - in_lanes(times(m3, g13))])
    four = of_four(t, ("yh", "yl"))
    t = (four[0] + four[1]) + (four[2] + four[3])
    m2 = mix(full2, t[0], partner(t[0], "xl"), "xl")
    four = of_four(t[1] - times(m2, g12), ("xh", "xl"))
    m1 = mix(full1, four[0] + four[1], four[2] + four[3], "xh")

    own = spread(jnp.concatenate([m4, m3, m2, m1], axis=0), "z", Z)
    other = partner(own, "c")
    m = jnp.stack([both_cores(own, other, 16 * n, 16) for n in (3, 2, 1, 0)])
    high = lax.reduce_precision(m, 8, 7)
    low = (m - high).astype(BF16)
    dims = ((0, 2), (0, 2))
    return x0 - (dot(left_basis, high.astype(BF16), dims) + dot(left_basis, low, dims))


def solution(mesh):
    fine = Mesh(mesh.devices.reshape(SIZES), AXES)
    row = P(AXES, None)
    level = P(None, AXES, None)
    return jax.shard_map(
        local,
        mesh=fine,
        in_specs=(row, row, level, level, row, row, row, row),
        out_specs=row,
        check_vma=False,
    )
```

```python
import jax
import jax.numpy as jnp
from jax import lax
from jax.experimental import pallas as pl
from jax.experimental.pallas import tpu as pltpu
from jax.sharding import Mesh, PartitionSpec as P

AXES = ("xh", "xl", "yh", "yl", "z", "c")
SIZES = (2, 2, 2, 2, 8, 2)
Z = 8
STEPS = 4
F32 = jnp.float32
BF16 = jnp.bfloat16
PAIRS = ((3, 4), (2, 4), (1, 4), (2, 3), (1, 3), (1, 2))
DIRECT = (4, (3, 4), (2, 4), (1, 4))
SHARED = (3, (2, 3), (1, 3), 2, 1, (1, 2))


def dot(a, b, dims):
    return lax.dot_general(a, b, ((dims[0], dims[1]), ((), ())), preferred_element_type=F32)


def fdot(a, b, dims):
    return lax.dot_general(
        a, b, ((dims[0], dims[1]), ((), ())), precision=lax.Precision.HIGH, preferred_element_type=F32
    )


def pack_kernel(a_ref, b_ref, c_ref, d_ref, out_ref):
    for z in range(Z):
        out_ref[z, 0:16, :] = a_ref[...]
        out_ref[z, 16:24, :] = b_ref[...]
        out_ref[z, 24:28, :] = c_ref[...]
        out_ref[z, 28:30, :] = d_ref[...]
        out_ref[z, 30:32, :] = jnp.zeros((2, 512), F32)


def pack(k4, k3, k2, k1):
    return pl.pallas_call(pack_kernel, out_shape=jax.ShapeDtypeStruct((Z, 32, 512), F32), name="pack")(k4, k3, k2, k1)


def leaf_kernel(
    core_ref, pair_ref, inv_hbm, rhs_hbm, v_hbm, w_hbm, x_hbm, keep_hbm, give_hbm, keep_shared_hbm, give_shared_hbm,
    x_ref, keep_ref, give_ref, keep_shared_ref, give_shared_ref, inv_ref, rhs_ref, v_ref, w_ref, high_ref, low_ref, sems,
):
    rows = 1024 // STEPS
    count = [0]

    def load(src, dst):
        copy = pltpu.make_async_copy(src, dst, sems.at[count[0]])
        count[0] += 1
        copy.start()
        return copy

    wait_w, wait_v = {}, {}
    wait_w[4] = load(w_hbm.at[3], w_ref.at[2])
    wait_v[3] = load(v_hbm.at[2], v_ref.at[2])
    wait_v[2] = load(v_hbm.at[1], v_ref.at[1])
    wait_v[1] = load(v_hbm.at[0], v_ref.at[0])
    wait_w[3] = load(w_hbm.at[2], w_ref.at[1])
    wait_w[2] = load(w_hbm.at[1], w_ref.at[0])
    wait_rhs = load(rhs_hbm, rhs_ref)
    parts = [pl.ds(step * rows, rows) for step in range(STEPS)]
    wait_inv = [load(inv_hbm.at[part], inv_ref.at[part]) for part in parts]
    wait_v[4] = load(v_hbm.at[3], v_ref.at[3])
    first_core = core_ref[0] == 0
    first_lanes = pair_ref[0] == 0

    def store(name, value):
        low, high = value[:128], value[128:]
        keep = jnp.where(first_core, low, high).reshape(Z, 16, 256)
        give = jnp.where(first_core, high, low).reshape(Z, 16, 256)
        if name in DIRECT:
            n = DIRECT.index(name)
            keep_ref[:, n] = keep
            give_ref[:, n] = give
            stores.append(load(give_ref.at[:, n], give_hbm.at[:, n]))
            stores.append(load(keep_ref.at[:, n], keep_hbm.at[:, n]))
            return
        n = SHARED.index(name)
        for value, ref in ((keep, keep_shared_ref), (give, give_shared_ref)):
            left, right = value[:, :, :128], value[:, :, 128:]
            ref[0, :, n] = jnp.where(first_lanes, left, right)
            ref[1, :, n] = jnp.where(first_lanes, right, left)
        stores.append(load(give_shared_ref.at[:, :, n], give_shared_hbm.at[:, :, n]))
        stores.append(load(keep_shared_ref.at[:, :, n], keep_shared_hbm.at[:, :, n]))

    stores = []
    done = set()

    def ready(waits, level):
        if (id(waits), level) not in done:
            done.add((id(waits), level))
            waits[level].wait()

    turned = {}
    for j, k in PAIRS:
        ready(wait_w, k)
        if k not in turned:
            turned[k] = w_ref[k - 2].T
        ready(wait_v, j)
        store((j, k), dot(turned[k], v_ref[j - 1], ((1,), (0,))))
    wait_rhs.wait()
    rhs = rhs_ref[...]
    rhs_turned = rhs.T
    for step, part in enumerate(parts):
        wait_inv[step].wait()
        inv = inv_ref[part, :]
        x_ref[part, :] = jnp.dot(inv, rhs, preferred_element_type=F32)
        stores.append(load(x_ref.at[part], x_hbm.at[part]))
        xt = dot(rhs_turned, inv, ((1,), (1,)))
        high = xt.astype(BF16)
        high_ref[:, part] = high
        low_ref[:, part] = (xt - high.astype(F32)).astype(BF16)
    for j in (4, 3, 2, 1):
        ready(wait_v, j)
        v = v_ref[j - 1]
        store(j, dot(high_ref[...], v, ((1,), (0,))) + dot(low_ref[...], v, ((1,), (0,))))
    for copy in stores:
        copy.wait()


def leaf(core, pair, leaf_inv, right_side, right_basis, left_basis):
    any_space = pl.BlockSpec(memory_space=pl.ANY)
    direct, shared = (Z, 4, 16, 256), (2, Z, 6, 16, 128)
    shapes = [(1024, 256), direct, direct, shared, shared]
    return pl.pallas_call(
        leaf_kernel,
        in_specs=[pl.BlockSpec(memory_space=pltpu.SMEM)] * 2 + [any_space] * 4,
        out_specs=[any_space] * 5,
        out_shape=[jax.ShapeDtypeStruct(shape, F32) for shape in shapes],
        scratch_shapes=[pltpu.VMEM(shape, F32) for shape in shapes]
        + [
            pltpu.VMEM((1024, 1024), BF16),
            pltpu.VMEM((1024, 256), BF16),
            pltpu.VMEM((4, 1024, 256), BF16),
            pltpu.VMEM((3, 1024, 256), BF16),
            pltpu.VMEM((256, 1024), BF16),
            pltpu.VMEM((256, 1024), BF16),
            pltpu.SemaphoreType.DMA((28 + 2 * STEPS,)),
        ],
        name="leaf",
    )(core.reshape(1), pair.reshape(1), leaf_inv, right_side, right_basis, left_basis)


def offsets(bit, step):
    return jnp.where(bit == 0, 0, step), jnp.where(bit == 0, step, 0)


def pair(core_ref, own, other):
    first = core_ref[0] == 0
    return jnp.where(first, own, other), jnp.where(first, other, own)


def fine_kernel(core_ref, yl_ref, rows, rows_c, a, a_c, k4_ref, k3_ref):
    near, far = offsets(yl_ref[0], 1)
    for z in range(Z):
        low, high = pair(core_ref, rows[z, 0:16], rows_c[z, 0:16])
        k4_ref[32 * z : 32 * z + 16] = low
        k4_ref[32 * z + 16 : 32 * z + 32] = high
        for t, own, other in ((near, rows[z, 16:24], rows_c[z, 16:24]), (far, a[z], a_c[z])):
            both = jnp.concatenate(pair(core_ref, own, other), axis=0)
            k3_ref[pl.ds(pl.multiple_of(128 * t + 16 * z, 16), 16)] = both


def coarse_kernel(core_ref, yl_ref, yh_ref, xl_ref, rows, rows_c, a, a_c, b, b_c, e, e_c, k2_ref, k1_ref):
    near, far = offsets(yl_ref[0], 1)
    up, down = offsets(yh_ref[0], 2)
    left, right = offsets(xl_ref[0], 4)

    def both(own, other):
        return jnp.concatenate(pair(core_ref, own, other), axis=0)

    for z in range(Z):
        for t, own, other in (
            (up + near, rows[z, 0:4], rows_c[z, 0:4]),
            (up + far, a[z, 0:4], a_c[z, 0:4]),
            (down + near, b[z, 0:4], b_c[z, 0:4]),
            (down + far, b[z, 8:12], b_c[z, 8:12]),
        ):
            k2_ref[pl.ds(pl.multiple_of(64 * t + 8 * z, 8), 8)] = both(own, other)
    for z in range(0, Z, 2):
        for t, (own, other, row) in (
            (left + up + near, (rows, rows_c, 4)),
            (left + up + far, (a, a_c, 4)),
            (left + down + near, (b, b_c, 4)),
            (left + down + far, (b, b_c, 12)),
            (right + up + near, (e, e_c, 0)),
            (right + up + far, (e, e_c, 2)),
            (right + down + near, (e, e_c, 4)),
            (right + down + far, (e, e_c, 6)),
        ):
            tile = [both(own[y, row : row + 2], other[y, row : row + 2]) for y in (z, z + 1)]
            k1_ref[pl.ds(pl.multiple_of(32 * t + 4 * z, 8), 8)] = jnp.concatenate(tile, axis=0)


def assemble(kernel, scalars, pieces, blocks):
    specs = [pl.BlockSpec((Z, count, 512), lambda i, index=index: (0, index, 0)) for count, index in blocks]
    full = pl.BlockSpec((256, 512), lambda i: (0, 0))
    return pl.pallas_call(
        kernel,
        grid=(1,),
        in_specs=[pl.BlockSpec(memory_space=pltpu.SMEM)] * len(scalars) + specs,
        out_specs=[full, full],
        out_shape=[jax.ShapeDtypeStruct((256, 512), F32)] * 2,
    )(*[scalar.reshape(1) for scalar in scalars], *pieces)


def partner(block, axis):
    return lax.ppermute(block, axis, [(0, 1), (1, 0)])


def ordered(bit, own, other, axis):
    low = jnp.where(bit == 0, own, other)
    high = jnp.where(bit == 0, other, own)
    return jnp.concatenate([low, high], axis=axis)


def exchange(block, axes):
    return lax.all_to_all(block, axes, 0, 0, tiled=True)


def spread(block, axes, count):
    return exchange(jnp.broadcast_to(block[None], (count,) + block.shape), axes)


def local(right_side, leaf_inv, right_basis, left_basis, k1, k2, k3, k4):
    at = {axis: lax.axis_index(axis) for axis in AXES}
    core = at["c"]
    rows = exchange(pack(k4, k3, k2, k1), "z")
    x0, keep, give, keep_shared, give_shared = leaf(
        core, at["yl"], leaf_inv, right_side, right_basis, left_basis
    )
    mine = partner(give, "c")
    mine = keep + mine
    got_shared = partner(give_shared, "c")
    got = partner(keep_shared[1] + got_shared[1], "yl")
    direct = exchange(mine, "z")
    pairs = (keep_shared[0] + got_shared[0]) + got
    pairs, rows = lax.optimization_barrier((pairs, rows))
    upper = at["yh"] == 0
    fours = pairs[:, 3:5]
    give = jnp.where(upper, fours[:, :, 8:], fours[:, :, :8]).reshape(Z, 1, 16, 128)
    got = partner(jnp.concatenate([give, pairs[:, 5:]], axis=1), "yh")
    keep = jnp.where(upper, fours[:, :, :8], fours[:, :, 8:]).reshape(Z, 1, 16, 128)
    fours = jnp.concatenate([keep, pairs[:, 5:]], axis=1) + got
    a0 = rows[:, 16:32]
    a1 = partner(a0, "yl")
    rows_c = partner(rows, "c")
    a1_c = partner(a1, "c")
    b0 = jnp.concatenate([a0[:, 8:], a1[:, 8:]], axis=1)
    b1 = partner(b0, "yh")
    b1_c = partner(b1, "c")
    e0 = jnp.concatenate([b0[:, 4:6], b0[:, 12:14], b1[:, 4:6], b1[:, 12:14]], axis=1)
    e1 = partner(e0, "xl")
    e1_c = partner(e1, "c")
    pieces = [rows, rows_c, a1, a1_c]
    full4, full3 = assemble(fine_kernel, [core, at["yl"]], pieces, [(32, 0)] * 2 + [(8, 0)] * 2)
    scalars = [at[axis] for axis in ("c", "yl", "yh", "xl")]
    full2, full1 = assemble(
        coarse_kernel, scalars, pieces + [b1, b1_c, e1, e1_c], [(8, 3)] * 2 + [(8, 1)] * 2 + [(16, 0)] * 2 + [(8, 0)] * 2
    )

    def both_cores(own, other, first, count):
        own = own[:, first : first + count].reshape(Z * count, -1)
        other = other[:, first : first + count].reshape(Z * count, -1)
        return ordered(core, own, other, 0)

    def mix(k, own, other, axis):
        return fdot(ordered(at[axis], own, other, 1), k, ((1,), (1,)))

    def of_four(block, axes):
        got = {}
        for k in (2, 1, 3):
            got[k] = lax.ppermute(block, axes, [(i, i ^ k) for i in range(4)])
        return [block, got[1], got[2], got[3]]

    def times(m, g):
        return fdot(m, g, ((1,), (0,)))

    def in_lanes(block):
        zero = jnp.zeros_like(block)
        first = at["yl"] == 0
        return jnp.concatenate([jnp.where(first, block, zero), jnp.where(first, zero, block)], axis=1)

    def in_rows(block):
        zero = jnp.zeros_like(block)
        return jnp.concatenate([jnp.where(upper, block, zero), jnp.where(upper, zero, block)], axis=0)

    direct = direct.sum(axis=0)
    to_all = jnp.broadcast_to(jnp.concatenate([direct[1:, :, :128], direct[1:, :, 128:]], axis=0)[None], (Z, 6, 16, 128))
    mixed = jnp.concatenate(
        [to_all.reshape(Z, 96, 128), pairs[:, :3].reshape(Z, 48, 128), fours.reshape(Z, 32, 128)], axis=1
    )
    mixed = exchange(mixed, "z")
    m4 = mix(full4, direct[0], partner(direct[0], "yl"), "yl")
    own = mixed[:, :96]
    other = partner(own, "c")
    g34, g24, g14 = [
        jnp.concatenate([both_cores(own, other, 16 * n, 16), both_cores(own, other, 48 + 16 * n, 16)], axis=1)
        for n in range(3)
    ]
    sums = mixed[:, 96:].sum(axis=0)
    third = spread(jnp.concatenate([sums[16:48], sums[64:80]], axis=0), "z", Z)
    t = in_lanes(sums[0:16]) - times(m4, g34)
    four = of_four(t, ("yh", "yl"))
    m3 = mix(full3, four[0] + four[1], four[2] + four[3], "yh")
    own, m3 = lax.optimization_barrier((third, m3))
    t2 = in_rows(in_lanes(sums[48:56])) - times(m4, g24)
    t1 = in_rows(in_lanes(sums[56:64])) - times(m4, g14)
    other = partner(own, "c")
    g23, g13 = both_cores(own, other, 0, 16), both_cores(own, other, 16, 16)
    half = both_cores(own, other, 32, 16)
    got = partner(half, "yl")
    g12 = ordered(at["yl"], half, got, 1)
    t = jnp.stack([t2 - in_lanes(times(m3, g23)), t1 - in_lanes(times(m3, g13))])
    four = of_four(t, ("yh", "yl"))
    t = (four[0] + four[1]) + (four[2] + four[3])
    m2 = mix(full2, t[0], partner(t[0], "xl"), "xl")
    four = of_four(t[1] - times(m2, g12), ("xh", "xl"))
    m1 = mix(full1, four[0] + four[1], four[2] + four[3], "xh")

    own = spread(jnp.concatenate([m4, m3, m2, m1], axis=0), "z", Z)
    other = partner(own, "c")
    m = jnp.stack([both_cores(own, other, 16 * n, 16) for n in (3, 2, 1, 0)])
    high = lax.reduce_precision(m, 8, 7)
    low = (m - high).astype(BF16)
    dims = ((0, 2), (0, 2))
    return x0 - (dot(left_basis, high.astype(BF16), dims) + dot(left_basis, low, dims))


def solution(mesh):
    fine = Mesh(mesh.devices.reshape(SIZES), AXES)
    row = P(AXES, None)
    level = P(None, AXES, None)
    return jax.shard_map(
        local,
        mesh=fine,
        in_specs=(row, row, level, level, row, row, row, row),
        out_specs=row,
        check_vma=False,
    )
```
